32 devices in a mesh: dp: 8 (over z, core), expert: 4 (over y, x).
Axes of the slice: x: 2, y: 2, z: 4, core: 2. Of those that a mesh axis runs over, the one named last changes fastest.
Arguments:
- tokens: bfloat16 [5120, 2048], P(('dp', 'expert')), may hold values from -6 to 6
- expert_ids: int32 [5120, 8], P(('dp', 'expert')), may hold values from 0 to 122, as said below
- gate_probs: float32 [5120, 8], P(('dp', 'expert')), may hold values from 0.02 to 1
- upstream: bfloat16 [5120, 2048], P(('dp', 'expert')), may hold values from -6 to 6
- w_gate: bfloat16 [4, 2048, 768], P('expert'), may hold values from -0.125 to 0.125
- w_up: bfloat16 [4, 2048, 768], P('expert'), may hold values from -0.125 to 0.125
- w_down: bfloat16 [4, 2048, 768], P('expert'), may hold values from -0.21875 to 0.21875
Outputs:
- layer_out: bfloat16 [5120, 2048], P(('dp', 'expert'))
- grad_tokens: bfloat16 [5120, 2048], P(('dp', 'expert'))
- grad_probs: float32 [5120, 8], P(('dp', 'expert'))
- grad_gate: float32 [4, 2048, 768], P('expert', 'dp')
- grad_up: float32 [4, 2048, 768], P('expert', 'dp')
- grad_down: float32 [4, 2048, 768], P('expert', 'dp')
The draws below stay inside these ranges and needn't reach their ends.
Inputs may be any that keep to these rules, and one draw needn't show every extreme that they name: `expert_ids`: slot 0 of every token names one of the experts 0 to 3, the experts computed here; slot k, for k from 1 to 7, names an expert from 4 + (k - 1) * 17 to 4 + k * 17 - 1. `expert_ids`: among the 160 tokens of one device, slot 0 names no expert more than 100 times; on every index of dp one expert is named by slot 0 exactly 100 times by the tokens of each device of that index.
All inputs are finite; a program needn't handle non-finite values.
Results may differ from the reference program's by a relative error of at most 0.0058.
Values may be sent and summed in bfloat16 or wider, within the bound.
A program may use at most 128 MiB of HBM per device.

```python
import math
import jax
import jax.numpy as jnp
from jax import lax

D = 2048
FF = 768
TOP = 8
TOK_DEV = 160
EXPERTS = 4
CAP = 100
GROUP = 17
TOKENS = 5120
N_DP = 8


def draw_expert_ids(key, part):
    blocks = TOKENS // TOK_DEV

    def one_block(block_index):
        row_key = jax.random.fold_in(jax.random.fold_in(key, 101), block_index // EXPERTS)
        hot_expert = jax.random.randint(row_key, (), 0, EXPERTS)
        block_key = jax.random.fold_in(jax.random.fold_in(key, 202), block_index)
        key_shuffle, key_jitter, key_others, key_later = jax.random.split(block_key, 4)
        shuffle = jax.random.permutation(key_shuffle, TOK_DEV)
        rank_in = jnp.argsort(shuffle).astype(jnp.int32)
        jitter = jax.random.randint(key_jitter, (TOK_DEV,), 0, 2)
        others = jax.random.permutation(key_others, EXPERTS - 1)
        other_slot = jnp.mod(rank_in - CAP + jitter, EXPERTS - 1)
        other_expert = jnp.mod(hot_expert + 1 + others[other_slot], EXPERTS)
        leading = jnp.where(rank_in < CAP, hot_expert, other_expert)
        later_slots = EXPERTS + jnp.arange(TOP - 1)[None, :] * GROUP + jax.random.randint(key_later, (TOK_DEV, TOP - 1), 0, GROUP)
        return jnp.concatenate([leading[:, None], later_slots], axis=1).astype(jnp.int32)
    return jax.vmap(one_block)(jnp.arange(blocks)).reshape(TOKENS, TOP).astype(jnp.int32)


def strengthened(drawn, own_key, source, target, shards_of, factor):
    def block_of(position):
        return (jnp.arange(drawn.shape[position]) // (drawn.shape[position] // shards_of)).reshape((-1,) + (1,) * (drawn.ndim - 1 - position))

    near = jax.random.permutation(own_key, shards_of)[block_of(target)]
    second = (block_of(target) + shards_of // 2) % shards_of
    return jnp.where((block_of(source) == near) | (block_of(source) == second), factor * drawn, drawn)


def shard_levels(own_key, dims, pieces, low, top_value):
    factor_of = 1.0
    for dim, parts in pieces:
        draws = jax.random.uniform(jax.random.fold_in(jax.random.fold_in(own_key, 6), dim), (parts,), jnp.float32, low / len(pieces), top_value / len(pieces))
        factor_of = factor_of * jnp.repeat(jnp.exp(draws), dims[dim] // parts).reshape((-1,) + (1,) * (len(dims) - 1 - dim))
    return factor_of


def normal_values(own_key, shape, deviation, limit, shards=(), kind=jnp.bfloat16):
    values = deviation * jax.random.normal(own_key, shape, jnp.float32)
    if shards:
        values = values * shard_levels(own_key, shape, shards, -0.22, 0.18)
    return jnp.clip(values, -limit, limit).astype(kind)


def noise_with(own_key, dims, deviation, limit, cuts, heavy, held_as=jnp.bfloat16):
    result = deviation * jax.random.normal(own_key, dims, jnp.float32)
    if cuts:
        result = result * shard_levels(own_key, dims, cuts, -0.22, 0.18)
    return jnp.clip(strengthened(result, jax.random.fold_in(own_key, 3), *heavy), -limit, limit).astype(held_as)


def setup_inputs(seed: int = 0) -> dict:
    key_of = jax.random.split(jax.random.key(seed), 8)
    tokens = noise_with(key_of[0], (TOKENS, D), 1.0, 6.0, ((0, 32),), (0, 1, 32, 2.75))
    expert_ids = draw_expert_ids(jax.random.fold_in(key_of[7], 71), 0)
    gate_probs = jnp.clip(jnp.exp(math.log(1.0) - 3.912023 * jax.random.uniform(key_of[2], (TOKENS, TOP), jnp.float32) ** shard_levels(key_of[2], (TOKENS, TOP), ((0, 32),), -0.2, 0.2)), 0.02, 1.0)
    upstream = normal_values(key_of[3], (TOKENS, D), 1.0, 6.0, ((0, 32),))
    w_gate = normal_values(key_of[4], (EXPERTS, D, FF), D ** -0.5, 0.125, ((0, 4),))
    w_up = normal_values(key_of[5], (EXPERTS, D, FF), D ** -0.5, 0.125, ((0, 4),))
    w_down = normal_values(key_of[6], (EXPERTS, D, FF), FF ** -0.5, 0.21875, ((0, 4),))
    return {"tokens": tokens, "expert_ids": expert_ids, "gate_probs": gate_probs, "upstream": upstream, "w_gate": w_gate, "w_up": w_up, "w_down": w_down}


def times_transposed(left, right):
    return lax.dot_general(left, right, (((1,), (1,)), ((), ())), preferred_element_type=jnp.float32)


def contract_rows(left, right):
    return lax.dot_general(left, right, (((0,), (0,)), ((), ())), preferred_element_type=jnp.float32)


def expert_pass(arrived, cot_rows, gate_mat, up_mat, down_mat):
    pre_gate = jnp.dot(arrived, gate_mat, preferred_element_type=jnp.float32)
    pre_up = jnp.dot(arrived, up_mat, preferred_element_type=jnp.float32)
    hidden = (pre_gate * jax.nn.sigmoid(pre_gate) * pre_up).astype(jnp.bfloat16)
    expert_out = times_transposed(hidden, down_mat).astype(jnp.bfloat16)
    grad_hidden = jnp.dot(cot_rows, down_mat, preferred_element_type=jnp.float32)
    sigmoid_gate = jax.nn.sigmoid(pre_gate)
    grad_pre_gate = (grad_hidden * pre_up * sigmoid_gate * (1.0 + pre_gate * (1.0 - sigmoid_gate))).astype(jnp.bfloat16)
    grad_pre_up = (grad_hidden * pre_gate * sigmoid_gate).astype(jnp.bfloat16)
    input_grad = (times_transposed(grad_pre_gate, gate_mat) + times_transposed(grad_pre_up, up_mat)).astype(jnp.bfloat16)
    return (expert_out, input_grad, contract_rows(arrived, grad_pre_gate),
            contract_rows(arrived, grad_pre_up), contract_rows(cot_rows, hidden))


def reference(tokens, expert_ids, gate_probs, upstream, w_gate, w_up, w_down):
    first_expert = expert_ids[:, 0].astype(jnp.int32)
    prob_total = jnp.sum(gate_probs, axis=1)
    gate_share = gate_probs[:, 0] / prob_total
    cotangent = (gate_share[:, None] * upstream.astype(jnp.float32)).astype(jnp.bfloat16)
    most_rows = N_DP * EXPERTS * CAP
    sorted_order = jnp.argsort(first_expert, stable=True).astype(jnp.int32)
    counts = jnp.sum((first_expert[:, None] == jnp.arange(EXPERTS, dtype=jnp.int32)[None, :]).astype(jnp.int32), axis=0)
    starts = (jnp.cumsum(counts) - counts).astype(jnp.int32)
    padded = jnp.concatenate([sorted_order, jnp.zeros((most_rows,), jnp.int32)])

    def one_expert(expert_index):
        row_index = lax.dynamic_slice(padded, (starts[expert_index],), (most_rows,))
        is_live = jnp.arange(most_rows, dtype=jnp.int32) < counts[expert_index]
        arrived = jnp.where(is_live[:, None], tokens[row_index], jnp.zeros((), tokens.dtype))
        cot_rows = jnp.where(is_live[:, None], cotangent[row_index], jnp.zeros((), cotangent.dtype))
        return expert_pass(arrived, cot_rows, w_gate[expert_index], w_up[expert_index], w_down[expert_index])

    outs_all, grads_all, grad_gate, grad_up, grad_down = lax.map(one_expert, jnp.arange(EXPERTS, dtype=jnp.int32))
    inverse = jnp.argsort(sorted_order).astype(jnp.int32)
    rank_in = (inverse - starts[first_expert]).astype(jnp.int32)
    mixed = outs_all[first_expert, rank_in]
    layer_out = (gate_share[:, None] * mixed.astype(jnp.float32)).astype(jnp.bfloat16)
    gate_product = jnp.sum(upstream.astype(jnp.float32) * mixed.astype(jnp.float32), axis=1)
    first_slot = (jnp.arange(TOP) == 0).astype(jnp.float32)
    grad_probs = (first_slot[None, :] - gate_share[:, None]) * (gate_product / prob_total)[:, None]
    grad_tokens = grads_all[first_expert, rank_in]
    return layer_out, grad_tokens, grad_probs, grad_gate, grad_up, grad_down
```

```python
import functools

import jax
import jax.numpy as jnp
from jax import lax
from jax.experimental import pallas as pl
from jax.experimental.pallas import tpu as pltpu
from jax.sharding import PartitionSpec as P

MESH = pl.DeviceIdType.MESH
F32 = jnp.float32
BF16 = jnp.bfloat16


def dot_nn(a, b):
    return lax.dot_general(a, b, (((1,), (0,)), ((), ())), preferred_element_type=F32)


def dot_nt(a, b):
    return lax.dot_general(a, b, (((1,), (1,)), ((), ())), preferred_element_type=F32)


def dot_tn(a, b):
    return lax.dot_general(a, b, (((0,), (0,)), ((), ())), preferred_element_type=F32)


def loop(count, body):
    def step(i, carry):
        body(i)
        return carry

    lax.fori_loop(0, count, step, 0)


def moe_kernel(
    owners, copies, cap,
    ids_ref, probs_ref, tok_ref, ups_ref, wg_hbm, wu_hbm, wd_hbm,
    out_ref, gtok_ref, gprob_ref, ggate_ref, gup_ref, gdown_ref,
    wg, wu, wd, onehot, xs, cs, xr, cr, ors, grs, pre_g, pre_u, hid, gpg, gpu,
    sib_s, sib_r, z_s, z_in, tmp,
    w_sem, x_ss, x_rs, c_ss, c_rs, o_ss, o_rs, g_ss, g_rs,
    sib_ss, sib_rs, z_ss, z_rs,
):
    me = lax.axis_index("expert")
    dp = lax.axis_index("dp")
    levels = copies // 2
    core = lax.rem(dp, 2)
    z = dp // 2
    tok_count, width = tok_ref.shape
    ff = hid.shape[1]
    rows = width // copies
    ft = 256
    dt = 256
    sibling = {"dp": dp + 1 - 2 * core}
    right = {"dp": lax.rem(dp + 2, copies)}
    left = {"dp": lax.rem(dp + copies - 2, copies)}

    w_copies = [
        pltpu.make_async_copy(src.at[0], dst, w_sem.at[i])
        for i, (src, dst) in enumerate(((wg_hbm, wg), (wu_hbm, wu), (wd_hbm, wd)))
    ]
    for copy in w_copies:
        copy.start()

    barrier = pltpu.get_barrier_semaphore()

    def greet(k):
        pl.semaphore_signal(
            barrier, inc=1, device_id={"expert": lax.rem(me + k + 1, owners)}, device_id_type=MESH
        )

    loop(owners - 1, greet)
    pl.semaphore_signal(barrier, inc=1, device_id=sibling, device_id_type=MESH)

    @pl.when(z > 0)
    def _():
        pl.semaphore_signal(barrier, inc=1, device_id=left, device_id_type=MESH)

    @pl.when(z < levels - 1)
    def _():
        pl.semaphore_signal(barrier, inc=1, device_id=right, device_id_type=MESH)

    ids = ids_ref[0:1, :]
    experts = lax.broadcasted_iota(jnp.int32, (max(owners, 8), tok_count), 0)
    match = (experts == ids).astype(BF16)
    before = (
        lax.broadcasted_iota(jnp.int32, (tok_count, tok_count), 0)
        < lax.broadcasted_iota(jnp.int32, (tok_count, tok_count), 1)
    ).astype(BF16)
    rank = jnp.sum(dot_nn(match, before) * match.astype(F32), axis=0, keepdims=True)
    target = ids * cap + rank.astype(jnp.int32)
    slots = lax.broadcasted_iota(jnp.int32, (owners * cap, tok_count), 0)
    onehot[...] = (slots == target).astype(BF16)

    probs = probs_ref[...]
    total = jnp.sum(probs, axis=0, keepdims=True)
    share_row = probs[0:1, :] / total
    share = jnp.transpose(jnp.broadcast_to(share_row, (8, tok_count)))[:, 0:1]

    def block(index):
        return pl.ds(pl.multiple_of(index * cap, 16), cap)

    def exchange(src, dst, ss, rs, k):
        peer = lax.rem(me + k + 1, owners)
        return pltpu.make_async_remote_copy(
            src_ref=src.at[block(peer)],
            dst_ref=dst.at[block(me)],
            send_sem=ss.at[k],
            recv_sem=rs.at[k],
            device_id={"expert": peer},
            device_id_type=MESH,
        )

    beside = (z + levels - 1) // levels + (2 * levels - 2 - z) // levels
    pl.semaphore_wait(barrier, owners + beside)

    def dispatch(values, src, dst, ss, rs):
        def one(k):
            peer = lax.rem(me + k + 1, owners)
            src[block(peer)] = dot_nn(onehot[block(peer)], values[...]).astype(BF16)
            exchange(src, dst, ss, rs, k).start()

        loop(owners - 1, one)
        dst[block(me)] = dot_nn(onehot[block(me)], values[...]).astype(BF16)

    dispatch(tok_ref, xs, xr, x_ss, x_rs)
    gtok_ref[...] = (share * ups_ref[...].astype(F32)).astype(BF16)

    upper = z // (levels // 2)
    chunk = 2 * rows

    def level_at(s):
        return upper * s + (1 - upper) * (levels - 1 - s)

    def cot_copy(s, k):
        peer = lax.rem(me + k + 1, owners)
        cols = pl.ds(pl.multiple_of(level_at(s) * chunk, 128), chunk)
        index = s * (owners - 1) + k
        return pltpu.make_async_remote_copy(
            src_ref=cs.at[block(peer), cols],
            dst_ref=cr.at[block(me), cols],
            send_sem=c_ss.at[index],
            recv_sem=c_rs.at[index],
            device_id={"expert": peer},
            device_id_type=MESH,
        )

    def send_chunk(s):
        cols = pl.ds(pl.multiple_of(level_at(s) * chunk, 128), chunk)
        cs[:, cols] = dot_nn(onehot[...], gtok_ref[:, cols]).astype(BF16)
        loop(owners - 1, lambda k: cot_copy(s, k).start())
        cr[block(me), cols] = cs[block(me), cols]

    loop(levels, send_chunk)

    w_copies[0].wait()
    w_copies[1].wait()
    loop(owners - 1, lambda k: exchange(xs, xr, x_ss, x_rs, k).wait_recv())

    def forward_tile(j):
        cols = pl.ds(pl.multiple_of(j * ft, 128), ft)
        a = dot_nn(xr[...], wg[:, cols])
        b = dot_nn(xr[...], wu[:, cols])
        pre_g[:, cols] = a
        pre_u[:, cols] = b
        hid[:, cols] = (a * jax.nn.sigmoid(a) * b).astype(BF16)

    loop(ff // ft, forward_tile)

    sides = ((cr, hid), (xr, gpg), (xr, gpu))

    def piece(m, dest):
        lhs, rhs = sides[m]
        cols = pl.ds(pl.multiple_of(dest * rows, 128), rows)
        return dot_tn(lhs[:, cols], rhs[...])

    def sib_copy(slot):
        return pltpu.make_async_remote_copy(
            src_ref=sib_s.at[slot], dst_ref=sib_r.at[slot],
            send_sem=sib_ss.at[slot], recv_sem=sib_rs.at[slot],
            device_id=sibling, device_id_type=MESH,
        )

    slots_all = 3 * levels

    def line_copy(slot, way):
        return pltpu.make_async_remote_copy(
            src_ref=z_s.at[slot], dst_ref=z_in.at[way * slots_all + slot],
            send_sem=z_ss.at[slot], recv_sem=z_rs.at[way * slots_all + slot],
            device_id={"dp": lax.rem(dp + 2 - 4 * way + copies, copies)}, device_id_type=MESH,
        )

    def to_sibling(m, s):
        level = level_at(s)
        slot = m * levels + level
        sib_s[slot] = piece(m, level * 2 + 1 - core).astype(BF16)
        sib_copy(slot).start()

    def chip_sum(m, level):
        slot = m * levels + level
        own = piece(m, level * 2 + core)
        sib_copy(slot).wait_recv()
        tmp[...] = own + sib_r[slot].astype(F32)

    def line_step(m, s, way):
        level = way * s + (1 - way) * (levels - 1 - s)
        slot = m * levels + level

        @pl.when((1 - 2 * way) * (level - z) > 0)
        def _():
            chip_sum(m, level)

            @pl.when(z * (1 - way) + (levels - 1 - z) * way > 0)
            def _():
                line_copy(slot, way).wait_recv()
                tmp[...] += z_in[way * slots_all + slot].astype(F32)

            z_s[slot] = tmp[...].astype(BF16)
            line_copy(slot, way).start()

    def toward(m, s):
        line_step(m, s, upper)

    def away(m, s):
        line_step(m, s, 1 - upper)

    def finish(m, dst):
        slot = m * levels + z

        @pl.when(z > 0)
        def _():
            line_copy(slot, 0).wait_recv()
            dst[0] += z_in[slot].astype(F32)

        @pl.when(z < levels - 1)
        def _():
            line_copy(slot, 1).wait_recv()
            dst[0] += z_in[slots_all + slot].astype(F32)

    edge = z * (levels - 1 - z) == 0

    def first_matrix(s):
        loop(owners - 1, lambda k: cot_copy(s, k).wait_recv())
        to_sibling(0, s)

        @pl.when(jnp.logical_and(edge, s > 0))
        def _():
            toward(0, s - 1)

    loop(levels, first_matrix)

    @pl.when(jnp.logical_not(edge))
    def _():
        toward(0, 0)

    w_copies[2].wait()
    loop(owners - 1, lambda k: exchange(xs, xr, x_ss, x_rs, k).wait_send())

    def out_tile(j):
        cols = pl.ds(pl.multiple_of(j * dt, 128), dt)
        xs[:, cols] = dot_nt(hid[...], wd[cols, :]).astype(BF16)

    loop(width // dt, out_tile)
    loop(owners - 1, lambda k: exchange(xs, ors, o_ss, o_rs, k).start())
    ors[block(me)] = xs[block(me)]

    def backward_tile(j):
        cols = pl.ds(pl.multiple_of(j * ft, 128), ft)
        grad = dot_nn(cr[...], wd[:, cols])
        a = pre_g[:, cols]
        s = jax.nn.sigmoid(a)
        gpg[:, cols] = (grad * pre_u[:, cols] * s * (1.0 + a * (1.0 - s))).astype(BF16)
        gpu[:, cols] = (grad * a * s).astype(BF16)

    loop(ff // ft, backward_tile)
    loop(levels, lambda s: to_sibling(1, s))

    @pl.when(edge)
    def _():
        loop(levels - 1, lambda s: toward(1, s))

    @pl.when(jnp.logical_not(edge))
    def _():
        loop(levels - 2, lambda s: toward(0, s + 1))

    loop(levels, lambda s: to_sibling(2, s))

    @pl.when(edge)
    def _():
        loop(levels - 1, lambda s: toward(2, s))

    @pl.when(jnp.logical_not(edge))
    def _():
        loop(levels - 1, lambda s: away(0, s))

    loop(levels, lambda s: loop(owners - 1, lambda k: cot_copy(s, k).wait_send()))

    def grad_tile(j):
        cols = pl.ds(pl.multiple_of(j * dt, 128), dt)
        cs[:, cols] = (dot_nt(gpg[...], wg[cols, :]) + dot_nt(gpu[...], wu[cols, :])).astype(BF16)

    loop(width // dt, grad_tile)
    loop(owners - 1, lambda k: exchange(cs, grs, g_ss, g_rs, k).start())
    grs[block(me)] = cs[block(me)]

    @pl.when(jnp.logical_not(edge))
    def _():
        for m in (1, 2):
            loop(levels - 1, lambda s: toward(m, s))
            loop(levels - 1, lambda s: away(m, s))

    for m, dst in enumerate((gdown_ref, ggate_ref, gup_ref)):
        chip_sum(m, z)
        dst[0] = tmp[...]

    loop(owners - 1, lambda k: exchange(xs, ors, o_ss, o_rs, k).wait_recv())
    product = jnp.zeros((tok_count, 1), F32)
    for j in range(width // dt):
        cols = pl.ds(j * dt, dt)
        mixed = dot_tn(onehot[...], ors[:, cols])
        out_ref[:, cols] = (share * mixed).astype(BF16)
        product += jnp.sum(ups_ref[:, cols].astype(F32) * mixed, axis=1, keepdims=True)
    first = (lax.broadcasted_iota(jnp.int32, probs.shape, 0) == 0).astype(F32)
    product_row = jnp.transpose(jnp.broadcast_to(product, (tok_count, 128)))[0:1, :]
    gprob_ref[...] = (first - share_row) * (product_row / total)

    loop(owners - 1, lambda k: exchange(cs, grs, g_ss, g_rs, k).wait_recv())

    def unpack_tile(j):
        cols = pl.ds(pl.multiple_of(j * dt, 128), dt)
        gtok_ref[:, cols] = dot_tn(onehot[...], grs[:, cols]).astype(BF16)

    loop(width // dt, unpack_tile)

    finish(0, gdown_ref)
    finish(1, ggate_ref)
    finish(2, gup_ref)

    loop(owners - 1, lambda k: exchange(xs, ors, o_ss, o_rs, k).wait_send())
    loop(owners - 1, lambda k: exchange(cs, grs, g_ss, g_rs, k).wait_send())
    loop(3 * levels, lambda slot: sib_copy(slot).wait_send())

    def sent(slot):
        @pl.when(lax.rem(slot, levels) != z)
        def _():
            line_copy(slot, 0).wait_send()

    loop(3 * levels, sent)


def copy_kernel(*refs):
    sems = refs[18]
    reads = [pltpu.make_async_copy(refs[i], refs[12 + i], sems.at[i]) for i in range(6)]
    writes = [pltpu.make_async_copy(refs[12 + i], refs[6 + i], sems.at[6 + i]) for i in range(6)]
    for move in reads:
        move.start()
    for read, write in zip(reads, writes):
        read.wait()
        write.start()
    for move in writes:
        move.wait()


def per_device(tokens, expert_ids, gate_probs, upstream, w_gate, w_up, w_down):
    tok_count, width = tokens.shape
    owners = lax.axis_size("expert")
    copies = lax.axis_size("dp")
    ff = w_gate.shape[2]
    capacity = tok_count // owners * 5 // 2
    cap = -(-capacity // CAP_ALIGN) * CAP_ALIGN
    slots = owners * cap
    levels = copies // 2
    rows = width // copies
    vmem = pl.BlockSpec(memory_space=pltpu.VMEM)
    hbm = pl.BlockSpec(memory_space=pl.ANY)
    dma = pltpu.SemaphoreType.DMA
    weight = pltpu.VMEM((width, ff), BF16)
    wide = pltpu.VMEM((slots, width), BF16)
    narrow = pltpu.VMEM((slots, ff), BF16)
    stack = pltpu.VMEM((3 * levels, rows, ff), BF16)
    grad = jax.ShapeDtypeStruct((1, rows, ff), F32)
    results = pl.pallas_call(
        functools.partial(moe_kernel, owners, copies, cap),
        out_shape=(
            jax.ShapeDtypeStruct((tok_count, width), BF16),
            jax.ShapeDtypeStruct((tok_count, width), BF16),
            jax.ShapeDtypeStruct(gate_probs.shape[::-1], F32),
            grad, grad, grad,
        ),
        in_specs=[vmem, vmem, vmem, vmem, hbm, hbm, hbm],
        out_specs=(vmem,) * 6,
        scratch_shapes=[
            weight, weight, weight,
            pltpu.VMEM((slots, tok_count), BF16),
            wide, wide, wide, wide, wide, wide,
            pltpu.VMEM((slots, ff), F32), pltpu.VMEM((slots, ff), F32),
            narrow, narrow, narrow,
            stack, stack, stack,
            pltpu.VMEM((6 * levels, rows, ff), BF16),
            pltpu.VMEM((rows, ff), F32),
            dma((3,)),
            dma((owners - 1,)), dma((owners - 1,)),
            dma((levels * (owners - 1),)), dma((levels * (owners - 1),)),
            *[dma((owners - 1,))] * 4,
            *[dma((3 * levels,))] * 3,
            dma((6 * levels,)),
        ],
        compiler_params=pltpu.CompilerParams(
            collective_id=0, has_side_effects=True, vmem_limit_bytes=62 * 2**20
        ),
    )(expert_ids.T, gate_probs.T, tokens, upstream, w_gate, w_up, w_down)
    layer_out, grad_tokens, grad_probs, grad_gate, grad_up, grad_down = pl.pallas_call(
        copy_kernel,
        out_shape=[jax.ShapeDtypeStruct(r.shape, r.dtype) for r in results],
        in_specs=[hbm] * 6,
        out_specs=[hbm] * 6,
        scratch_shapes=[pltpu.VMEM(r.shape, r.dtype) for r in results] + [dma((12,))],
    )(*results)
    return (layer_out, grad_tokens, grad_probs.T, grad_gate, grad_up, grad_down)


CAP_ALIGN = 16


def solution(mesh):
    rows = P(("dp", "expert"), None)
    experts = P("expert", None, None)
    grads = P("expert", "dp", None)
    return jax.shard_map(
        per_device,
        mesh=mesh,
        in_specs=(rows, rows, rows, rows, experts, experts, experts),
        out_specs=(rows, rows, rows, grads, grads, grads),
        check_vma=False,
    )
```

```python
import functools

import jax
import jax.numpy as jnp
from jax import lax
from jax.experimental import pallas as pl
from jax.experimental.pallas import tpu as pltpu
from jax.sharding import PartitionSpec as P

MESH = pl.DeviceIdType.MESH
F32 = jnp.float32
BF16 = jnp.bfloat16


def dot_nn(a, b):
    return lax.dot_general(a, b, (((1,), (0,)), ((), ())), preferred_element_type=F32)


def dot_nt(a, b):
    return lax.dot_general(a, b, (((1,), (1,)), ((), ())), preferred_element_type=F32)


def dot_tn(a, b):
    return lax.dot_general(a, b, (((0,), (0,)), ((), ())), preferred_element_type=F32)


def loop(count, body):
    def step(i, carry):
        body(i)
        return carry

    lax.fori_loop(0, count, step, 0)


def moe_kernel(
    owners, copies, base, rem, parts,
    ids_ref, probs_ref, tok_ref, ups_ref, wg_hbm, wu_hbm, wd_hbm,
    out_ref, gtok_ref, gprob_ref, ggate_ref, gup_ref, gdown_ref,
    wg, wu, wd, hot, hot_rem, back, back_rem,
    xs, cs, xr, cr, xe, ors, grs, rem_s, rem_r, xt, ct, xet,
    pre_g, pre_u, hid, gpre, gedge,
    sib_s, sib_r, z_s, z_in, tmp,
    w_sem, x_ss, x_rs, c_ss, c_rs, o_ss, o_rs, g_ss, g_rs, r_ss, r_rs,
    xe_ss, xe_rs, ge_ss, ge_rs, sib_ss, sib_rs, z_ss, z_rs,
):
    me = lax.axis_index("expert")
    dp = lax.axis_index("dp")
    levels = copies // 2
    core = lax.rem(dp, 2)
    z = dp // 2
    tok_count, width = tok_ref.shape
    ff = hid.shape[1]
    rows = width // copies
    chunk = 2 * rows
    main = owners * base
    groups = PACK // rem if rem else 1
    group = width // groups
    ft = 256
    pw = ff // parts
    others = owners - 1
    sibling = {"dp": dp + 1 - 2 * core}
    right = {"dp": lax.rem(dp + 2, copies)}
    left = {"dp": lax.rem(dp + copies - 2, copies)}
    upper = z // (levels // 2)
    ahead = {"dp": lax.rem(dp + 2 - 4 * upper + copies, copies)}
    edge = z * (levels - 1 - z) == 0
    n_toward = upper * z + (1 - upper) * (levels - 1 - z)
    n_away = levels - 1 - n_toward

    def near_edge(body):
        if levels == 4:
            body()
        else:
            pl.when((z - 1) * (levels - 2 - z) == 0)(body)

    def far_from_edge(body):
        if levels > 4:
            pl.when((z - 1) * (levels - 2 - z) != 0)(body)

    w_copies = [
        pltpu.make_async_copy(src.at[0], dst, w_sem.at[i])
        for i, (src, dst) in enumerate(((wg_hbm, wg), (wu_hbm, wu), (wd_hbm, wd)))
    ]
    for copy in w_copies:
        copy.start()

    barrier = pltpu.get_barrier_semaphore()

    def greet(k):
        pl.semaphore_signal(
            barrier, inc=1, device_id={"expert": lax.rem(me + k + 1, owners)}, device_id_type=MESH
        )

    loop(others, greet)
    pl.semaphore_signal(barrier, inc=1, device_id=sibling, device_id_type=MESH)

    @pl.when(z > 0)
    def _():
        pl.semaphore_signal(barrier, inc=1, device_id=left, device_id_type=MESH)

    @pl.when(z < levels - 1)
    def _():
        pl.semaphore_signal(barrier, inc=1, device_id=right, device_id_type=MESH)

    ids = ids_ref[0:1, :]
    experts = lax.broadcasted_iota(jnp.int32, (max(owners, 8), tok_count), 0)
    match = (experts == ids).astype(BF16)
    before = (
        lax.broadcasted_iota(jnp.int32, (tok_count, tok_count), 0)
        < lax.broadcasted_iota(jnp.int32, (tok_count, tok_count), 1)
    ).astype(BF16)
    rank = jnp.sum(dot_nn(match, before) * match.astype(F32), axis=0, keepdims=True).astype(jnp.int32)
    target = jnp.where(rank < base, ids * base + rank, -1)
    hot[...] = (lax.broadcasted_iota(jnp.int32, (main, tok_count), 0) == target).astype(BF16)
    target_rem = jnp.where(rank < base, -PACK, ids * PACK + rank - base)
    if rem:
        slots = lax.broadcasted_iota(jnp.int32, (owners * PACK, tok_count), 0)
        for g in range(groups):
            hot_rem[g] = (slots == target_rem + g * rem).astype(BF16)

    probs = probs_ref[...]
    total = jnp.sum(probs, axis=0, keepdims=True)
    share_row = probs[0:1, :] / total

    def column(row):
        return jnp.transpose(jnp.broadcast_to(row, (8, tok_count)))[:, 0:1]

    share = column(share_row)

    def block(index):
        return pl.ds(pl.multiple_of(index * base, 16), base)

    def packed(index):
        return pl.ds(pl.multiple_of(index * PACK, 16), PACK)

    def level_at(s):
        return upper * s + (1 - upper) * (levels - 1 - s)

    def level_cols(level):
        return pl.ds(pl.multiple_of(level * chunk, 128), chunk)

    def block_copy(src, dst, ss, rs, s, k):
        peer = lax.rem(me + k + 1, owners)
        cols = level_cols(level_at(s))
        index = s * others + k
        return pltpu.make_async_remote_copy(
            src_ref=src.at[block(peer), cols],
            dst_ref=dst.at[block(me), cols],
            send_sem=ss.at[index],
            recv_sem=rs.at[index],
            device_id={"expert": peer},
            device_id_type=MESH,
        )

    def packed_copy(e, k):
        peer = lax.rem(me + k + 1, owners)
        return pltpu.make_async_remote_copy(
            src_ref=rem_s.at[e, packed(peer)],
            dst_ref=rem_r.at[e, packed(me)],
            send_sem=r_ss.at[e * others + k],
            recv_sem=r_rs.at[e * others + k],
            device_id={"expert": peer},
            device_id_type=MESH,
        )

    def send_packed(e, value):
        rem_s[e] = value.astype(BF16)
        loop(others, lambda k: packed_copy(e, k).start())
        rem_r[e, packed(me)] = rem_s[e, packed(me)]

    def dispatch_packed(e, values):
        if rem:
            send_packed(e, sum(
                dot_nn(hot_rem[g], values[:, g * group:(g + 1) * group]) for g in range(groups)
            ))

    def packed_match(g, shape, flat, wide):
        i = lax.broadcasted_iota(jnp.int32, shape, flat)
        j = lax.broadcasted_iota(jnp.int32, shape, wide)
        shift = rem.bit_length() - 1
        return (j == (i >> shift) * PACK + g * rem + (i & (rem - 1))).astype(BF16)

    def spread_packed(e, dst):
        if rem:
            loop(others, lambda k: packed_copy(e, k).wait_recv())
            arrived = rem_r[e]
            for g in range(groups):
                pick = packed_match(g, (owners * rem, owners * PACK), 0, 1)
                dst[main:main + owners * rem, g * group:(g + 1) * group] = dot_nn(pick, arrived).astype(BF16)

    def collect_packed(e, src):
        if rem:
            send_packed(e, sum(
                dot_nn(
                    packed_match(g, (owners * PACK, owners * rem), 1, 0),
                    src[main:main + owners * rem, g * group:(g + 1) * group],
                )
                for g in range(groups)
            ))

    def send_chunk(values, src, dst, ss, rs, s):
        cols = level_cols(level_at(s))
        src[0:main, cols] = dot_nn(hot[...], values[:, cols]).astype(BF16)
        loop(others, lambda k: block_copy(src, dst, ss, rs, s, k).start())
        dst[block(me), cols] = src[block(me), cols]

    beside = (z + levels - 1) // levels + (2 * levels - 2 - z) // levels
    pl.semaphore_wait(barrier, owners + beside)

    dispatch_packed(0, tok_ref)
    loop(levels, lambda s: send_chunk(tok_ref, xs, xr, x_ss, x_rs, s))
    gtok_ref[...] = (share * ups_ref[...].astype(F32)).astype(BF16)
    dispatch_packed(1, gtok_ref)
    loop(levels, lambda s: send_chunk(gtok_ref, cs, cr, c_ss, c_rs, s))

    place = lax.broadcasted_iota(jnp.int32, (tok_count, main), 1)
    back[...] = (place == column(target.astype(F32)).astype(jnp.int32)).astype(BF16)
    if rem:
        place = lax.broadcasted_iota(jnp.int32, (tok_count, owners * PACK), 1)
        target_col = column(target_rem.astype(F32)).astype(jnp.int32)
        for g in range(groups):
            back_rem[g] = (place == target_col + g * rem).astype(BF16)
    pre_g[...] = jnp.zeros_like(pre_g)
    pre_u[...] = jnp.zeros_like(pre_u)

    def edge_x_copy(s):
        cols = level_cols(level_at(s))
        return pltpu.make_async_remote_copy(
            src_ref=xr.at[:, cols], dst_ref=xe.at[:, cols],
            send_sem=xe_ss.at[s], recv_sem=xe_rs.at[s],
            device_id=ahead, device_id_type=MESH,
        )

    def part(p):
        return pl.ds(pl.multiple_of(p * pw, 128), pw)

    def edge_g_copy(p, i):
        return pltpu.make_async_remote_copy(
            src_ref=gpre.at[i, :, part(p)], dst_ref=gedge.at[i, :, part(p)],
            send_sem=ge_ss.at[p * 2 + i], recv_sem=ge_rs.at[p * 2 + i],
            device_id=ahead, device_id_type=MESH,
        )

    w_copies[0].wait()
    w_copies[1].wait()
    spread_packed(0, xr)

    def arrive_x(s):
        loop(others, lambda k: block_copy(xs, xr, x_ss, x_rs, s, k).wait_recv())

        @pl.when(jnp.logical_and(edge, s < levels - 2))
        def _():
            edge_x_copy(s).start()

    def flip(src, dst, s):
        level = level_at(s)
        dst[pl.ds(pl.multiple_of(level * chunk, 128), chunk), :] = jnp.transpose(src[:, level_cols(level)])

    def forward_chunk(s):
        arrive_x(s)
        depth = level_cols(level_at(s))

        def tile(j):
            cols = pl.ds(pl.multiple_of(j * ft, 128), ft)
            pre_g[:, cols] += dot_nn(xr[:, depth], wg[depth, cols])
            pre_u[:, cols] += dot_nn(xr[:, depth], wu[depth, cols])

        loop(ff // ft, tile)
        flip(xr, xt, s)

    loop(levels - 1, forward_chunk)
    arrive_x(levels - 1)
    last = level_cols(level_at(levels - 1))

    def forward_last(j):
        cols = pl.ds(pl.multiple_of(j * ft, 128), ft)
        a = pre_g[:, cols] + dot_nn(xr[:, last], wg[last, cols])
        b = pre_u[:, cols] + dot_nn(xr[:, last], wu[last, cols])
        pre_g[:, cols] = a
        pre_u[:, cols] = b
        hid[:, cols] = (a * jax.nn.sigmoid(a) * b).astype(BF16)

    loop(ff // ft, forward_last)

    def own_rows(dest):
        return pl.ds(pl.multiple_of(dest * rows, 128), rows)

    def piece(m, dest, cols):
        if m == 0:
            return dot_nn(ct[own_rows(dest), :], hid[:, cols])
        return dot_nn(xt[own_rows(dest), :], gpre[m - 1, :, cols])

    def edge_piece(m, dest, cols):
        return dot_nn(xet[own_rows(dest), :], gedge[m - 1, :, cols])

    def sib_copy(slot, p=None):
        if p is None:
            src, dst, index = sib_s.at[slot], sib_r.at[slot], slot * parts
        else:
            src, dst, index = sib_s.at[slot, :, part(p)], sib_r.at[slot, :, part(p)], slot * parts + p
        return pltpu.make_async_remote_copy(
            src_ref=src, dst_ref=dst,
            send_sem=sib_ss.at[index], recv_sem=sib_rs.at[index],
            device_id=sibling, device_id_type=MESH,
        )

    slots_all = 3 * levels

    def landing(slot, way, level):
        spare = jnp.where(lax.rem(slot, levels) == level, slots_all + slot // levels, slot)
        return way * spare + (1 - way) * slot

    def line_copy(slot, p, way, level=None):
        index = landing(slot, way, z + 1 - 2 * way if level is None else level)
        return pltpu.make_async_remote_copy(
            src_ref=z_s.at[slot, :, part(p)], dst_ref=z_in.at[index, :, part(p)],
            send_sem=z_ss.at[slot * parts + p],
            recv_sem=z_rs.at[index * parts + p],
            device_id={"dp": lax.rem(dp + 2 - 4 * way + copies, copies)}, device_id_type=MESH,
        )

    def sib_whole(m, level):
        slot = m * levels + level

        def one(p):
            sib_s[slot, :, part(p)] = piece(m, level * 2 + 1 - core, part(p)).astype(BF16)

        loop(parts, one)
        sib_copy(slot).start()

    def sib_part(m, level, p):
        slot = m * levels + level
        dest = level * 2 + 1 - core
        tmp[...] = piece(m, dest, part(p))

        @near_edge
        def _():
            tmp[...] += edge_piece(m, dest, part(p))

        sib_s[slot, :, part(p)] = tmp[...].astype(BF16)
        sib_copy(slot, p).start()

    def add_line(slot, p, way):
        line_copy(slot, p, way, z).wait_recv()
        tmp[...] += z_in[landing(slot, way, z), :, part(p)].astype(F32)

    def push(slot, p, way):
        z_s[slot, :, part(p)] = tmp[...].astype(BF16)
        line_copy(slot, p, way).start()

    def level_of(s, way):
        return way * s + (1 - way) * (levels - 1 - s)

    def whole_push(m, s, way, upstream, wait_sib=True, only=None):
        level = level_of(s, way)
        slot = m * levels + level
        if wait_sib:
            sib_copy(slot).wait_recv()

        def one(p):
            tmp[...] = piece(m, level * 2 + core, part(p)) + sib_r[slot, :, part(p)].astype(F32)
            if upstream:
                add_line(slot, p, way)
            push(slot, p, way)

        if only is None:
            loop(parts, one)
        else:
            one(only)

    def part_push(m, s, p):
        level = level_of(s, upper)
        slot = m * levels + level
        dest = level * 2 + core
        tmp[...] = piece(m, dest, part(p))

        @near_edge
        def _():
            tmp[...] += edge_piece(m, dest, part(p))

        @far_from_edge
        def _():
            add_line(slot, p, upper)

        sib_copy(slot, p).wait_recv()
        tmp[...] += sib_r[slot, :, part(p)].astype(F32)
        push(slot, p, upper)

    grads = (gdown_ref, ggate_ref, gup_ref)

    def own_sum(m):
        slot = m * levels + z
        sib_copy(slot).wait_recv()

        def one(p):
            grads[m][0, :, part(p)] = piece(m, z * 2 + core, part(p)) + sib_r[slot, :, part(p)].astype(F32)

        loop(parts, one)

    def own_part(m, p):
        slot = m * levels + z
        tmp[...] = piece(m, z * 2 + core, part(p))

        @near_edge
        def _():
            tmp[...] += edge_piece(m, z * 2 + core, part(p))

        sib_copy(slot, p).wait_recv()
        grads[m][0, :, part(p)] = tmp[...] + sib_r[slot, :, part(p)].astype(F32)

    def finish_way(m, way):
        slot = m * levels + z

        def one(p):
            line_copy(slot, p, way, z).wait_recv()
            grads[m][0, :, part(p)] += z_in[landing(slot, way, z), :, part(p)].astype(F32)

        loop(parts, one)

    w_copies[2].wait()
    loop(levels, lambda s: loop(others, lambda k: block_copy(xs, xr, x_ss, x_rs, s, k).wait_send()))

    def out_tile(j):
        cols = pl.ds(pl.multiple_of(j * ft, 128), ft)
        xs[:, cols] = dot_nt(hid[...], wd[cols, :]).astype(BF16)

    loop(width // ft, out_tile)
    ors[block(me)] = xs[block(me)]
    flip(xr, xt, levels - 1)
    spread_packed(1, cr)

    def stage(s):
        loop(others, lambda k: block_copy(cs, cr, c_ss, c_rs, s, k).wait_recv())
        flip(cr, ct, s)
        sib_whole(0, level_at(s))

        @pl.when(jnp.logical_and(edge, s < levels - 2))
        def _():
            whole_push(0, s, upper, False)

        @pl.when(jnp.logical_and(jnp.logical_not(edge), s == 0))
        def _():
            whole_push(0, s, upper, True)

    loop(levels, stage)

    collect_packed(2, xs)
    loop(levels, lambda s: loop(others, lambda k: block_copy(xs, ors, o_ss, o_rs, s, k).start()))

    def backward_tile(j):
        cols = pl.ds(pl.multiple_of(j * ft, 128), ft)
        grad = dot_nn(cr[...], wd[:, cols])
        a = pre_g[:, cols]
        s = jax.nn.sigmoid(a)
        gpre[0, :, cols] = (grad * pre_u[:, cols] * s * (1.0 + a * (1.0 - s))).astype(BF16)
        gpre[1, :, cols] = (grad * a * s).astype(BF16)

    loop(ff // ft, backward_tile)

    @pl.when(edge)
    def _():
        def one(p):
            edge_g_copy(p, 0).start()
            edge_g_copy(p, 1).start()

        loop(parts, one)

    @pl.when(jnp.logical_not(edge))
    def _():
        def later(s):
            @pl.when(s > 0)
            def _():
                whole_push(0, s, upper, True)

        loop(n_toward, later)

    loop(levels, lambda s: loop(others, lambda k: block_copy(cs, cr, c_ss, c_rs, s, k).wait_send()))

    def input_grad(s):
        def tile(j):
            cols = pl.ds(pl.multiple_of(level_at(s) * chunk + j * rows, 128), rows)
            cs[:, cols] = (dot_nt(gpre[0], wg[cols, :]) + dot_nt(gpre[1], wu[cols, :])).astype(BF16)

        loop(2, tile)
        loop(others, lambda k: block_copy(cs, grs, g_ss, g_rs, s, k).start())

    loop(levels, input_grad)
    collect_packed(3, cs)
    grs[block(me)] = cs[block(me)]

    @pl.when(edge)
    def _():
        sib_whole(1, z)
        sib_whole(2, z)

    @pl.when(jnp.logical_not(edge))
    def _():
        def away(s):
            level = level_of(s, 1 - upper)
            sib_whole(1, level)
            sib_whole(2, level)

        loop(n_away, away)

        @near_edge
        def _():
            def one(s):
                edge_x_copy(s).wait_recv()
                flip(xe, xet, s)

            loop(n_toward, one)

        loop(n_away, lambda s: whole_push(0, s, 1 - upper, True))

    own_sum(0)

    def tile_of(src, e, cols, g, offset):
        value = dot_nn(back[...], src[:, cols])
        if rem:
            value += dot_nn(back_rem[g], rem_r[e, :, offset:offset + ft])
        return value

    def take_out():
        if rem:
            loop(others, lambda k: packed_copy(2, k).wait_recv())
        loop(levels, lambda s: loop(others, lambda k: block_copy(xs, ors, o_ss, o_rs, s, k).wait_recv()))
        product = jnp.zeros((tok_count, 1), F32)
        for j in range(width // ft):
            cols = pl.ds(j * ft, ft)
            mixed = tile_of(ors, 2, cols, j * ft // group, j * ft % group)
            out_ref[:, cols] = (share * mixed).astype(BF16)
            product += jnp.sum(ups_ref[:, cols].astype(F32) * mixed, axis=1, keepdims=True)
        first = (lax.broadcasted_iota(jnp.int32, probs.shape, 0) == 0).astype(F32)
        product_row = jnp.transpose(jnp.broadcast_to(product, (tok_count, 128)))[0:1, :]
        gprob_ref[...] = (first - share_row) * (product_row / total)

    def take_input_grad():
        if rem:
            loop(others, lambda k: packed_copy(3, k).wait_recv())
        loop(levels, lambda s: loop(others, lambda k: block_copy(cs, grs, g_ss, g_rs, s, k).wait_recv()))
        for j in range(width // ft):
            cols = pl.ds(j * ft, ft)
            gtok_ref[:, cols] = tile_of(grs, 3, cols, j * ft // group, j * ft % group).astype(BF16)

    def toward_part(p):
        @pl.when(jnp.logical_not(edge))
        def _():
            @near_edge
            def _():
                edge_g_copy(p, 0).wait_recv()
                edge_g_copy(p, 1).wait_recv()

            def send(s):
                for m in (1, 2):
                    sib_part(m, level_of(s, upper), p)

            def onward(s):
                for m in (1, 2):
                    part_push(m, s, p)

            loop(n_toward, send)
            loop(n_toward, onward)

    def away_part(p):
        @pl.when(jnp.logical_not(edge))
        def _():
            def one(s):
                for m in (1, 2):
                    whole_push(m, s, 1 - upper, True, p == 0, p)

            loop(n_away, one)

    toward_part(0)

    @pl.when(edge)
    def _():
        own_sum(1)
        own_sum(2)

    take_out()

    for p in range(1, parts):
        toward_part(p)
        away_part(p - 1)

    @pl.when(edge)
    def _():
        def one(p):
            edge_g_copy(p, 0).wait_send()
            edge_g_copy(p, 1).wait_send()

        loop(parts, one)
        edge_x_copy(levels - 2).start()
        whole_push(0, levels - 2, upper, False)

    take_input_grad()

    @pl.when(jnp.logical_not(edge))
    def _():
        @near_edge
        def _():
            edge_x_copy(levels - 2).wait_recv()
            flip(xe, xet, levels - 2)

        for m in (1, 2):
            loop(parts, lambda p: sib_part(m, z, p))
        for m in (1, 2):
            loop(parts, lambda p: own_part(m, p))

    away_part(parts - 1)

    @pl.when(edge)
    def _():
        for m in range(3):
            finish_way(m, 1 - upper)

    @pl.when(jnp.logical_not(edge))
    def _():
        finish_way(0, upper)

        @far_from_edge
        def _():
            finish_way(1, upper)
            finish_way(2, upper)

        for m in range(3):
            finish_way(m, 1 - upper)

    loop(levels, lambda s: loop(others, lambda k: block_copy(xs, ors, o_ss, o_rs, s, k).wait_send()))
    loop(levels, lambda s: loop(others, lambda k: block_copy(cs, grs, g_ss, g_rs, s, k).wait_send()))
    if rem:
        loop(4, lambda e: loop(others, lambda k: packed_copy(e, k).wait_send()))
    loop(levels, lambda slot: sib_copy(slot).wait_send())

    def sent(m, level):
        @pl.when(level != z)
        def _():
            loop(parts, lambda p: line_copy(m * levels + level, p, 0).wait_send())

    loop(levels, lambda level: sent(0, level))

    @pl.when(edge)
    def _():
        sib_copy(levels + z).wait_send()
        sib_copy(2 * levels + z).wait_send()
        loop(levels - 1, lambda s: edge_x_copy(s).wait_send())

    @pl.when(jnp.logical_not(edge))
    def _():
        for m in (1, 2):
            loop(levels, lambda level: sent(m, level))
            loop(n_away, lambda s: sib_copy(m * levels + level_of(s, 1 - upper)).wait_send())
            loop(n_toward + 1, lambda s: loop(
                parts, lambda p: sib_copy(m * levels + level_of(s, upper), p).wait_send()
            ))


def copy_kernel(*refs):
    sems = refs[18]
    reads = [pltpu.make_async_copy(refs[i], refs[12 + i], sems.at[i]) for i in range(6)]
    writes = [pltpu.make_async_copy(refs[12 + i], refs[6 + i], sems.at[6 + i]) for i in range(6)]
    for move in reads:
        move.start()
    for read, write in zip(reads, writes):
        read.wait()
        write.start()
    for move in writes:
        move.wait()


def per_device(tokens, expert_ids, gate_probs, upstream, w_gate, w_up, w_down):
    tok_count, width = tokens.shape
    owners = lax.axis_size("expert")
    copies = lax.axis_size("dp")
    ff = w_gate.shape[2]
    capacity = tok_count // owners * 5 // 2
    rem = capacity % 16
    if rem == 0 or PACK % rem or (owners * rem) % 16:
        rem = 0
    base = capacity - rem if rem else -(-capacity // 16) * 16
    main = owners * base
    slots = main + owners * rem
    groups = PACK // rem if rem else 1
    levels = copies // 2
    rows = width // copies
    parts = PARTS
    others = owners - 1
    vmem = pl.BlockSpec(memory_space=pltpu.VMEM)
    hbm = pl.BlockSpec(memory_space=pl.ANY)
    dma = pltpu.SemaphoreType.DMA
    weight = pltpu.VMEM((width, ff), BF16)
    wide = pltpu.VMEM((slots, width), BF16)
    back = pltpu.VMEM((main, width), BF16)
    turned = pltpu.VMEM((width, slots), BF16)
    narrow = pltpu.VMEM((slots, ff), BF16)
    stack = pltpu.VMEM((3 * levels, rows, ff), BF16)
    packed = pltpu.VMEM((4, owners * PACK, width // groups), BF16)
    grad = jax.ShapeDtypeStruct((1, rows, ff), F32)
    results = pl.pallas_call(
        functools.partial(moe_kernel, owners, copies, base, rem, parts),
        out_shape=(
            jax.ShapeDtypeStruct((tok_count, width), BF16),
            jax.ShapeDtypeStruct((tok_count, width), BF16),
            jax.ShapeDtypeStruct(gate_probs.shape[::-1], F32),
            grad, grad, grad,
        ),
        in_specs=[vmem, vmem, vmem, vmem, hbm, hbm, hbm],
        out_specs=(vmem,) * 6,
        scratch_shapes=[
            weight, weight, weight,
            pltpu.VMEM((main, tok_count), BF16),
            pltpu.VMEM((groups, owners * PACK, tok_count), BF16),
            pltpu.VMEM((tok_count, main), BF16),
            pltpu.VMEM((groups, tok_count, owners * PACK), BF16),
            wide, wide, wide, wide, wide, back, back,
            packed, packed,
            turned, turned, turned,
            pltpu.VMEM((slots, ff), F32), pltpu.VMEM((slots, ff), F32),
            narrow, pltpu.VMEM((2, slots, ff), BF16), pltpu.VMEM((2, slots, ff), BF16),
            stack, stack, stack,
            pltpu.VMEM((3 * levels + 3, rows, ff), BF16),
            pltpu.VMEM((rows, ff // parts), F32),
            dma((3,)),
            *[dma((levels * others,))] * 8,
            dma((4 * others,)), dma((4 * others,)),
            dma((levels,)), dma((levels,)),
            dma((2 * parts,)), dma((2 * parts,)),
            *[dma((3 * levels * parts,))] * 3,
            dma(((3 * levels + 3) * parts,)),
        ],
        compiler_params=pltpu.CompilerParams(
            collective_id=0, has_side_effects=True, vmem_limit_bytes=62 * 2**20
        ),
    )(expert_ids.T, gate_probs.T, tokens, upstream, w_gate, w_up, w_down)
    layer_out, grad_tokens, grad_probs, grad_gate, grad_up, grad_down = pl.pallas_call(
        copy_kernel,
        out_shape=[jax.ShapeDtypeStruct(r.shape, r.dtype) for r in results],
        in_specs=[hbm] * 6,
        out_specs=[hbm] * 6,
        scratch_shapes=[pltpu.VMEM(r.shape, r.dtype) for r in results] + [dma((12,))],
    )(*results)
    return (layer_out, grad_tokens, grad_probs.T, grad_gate, grad_up, grad_down)


PACK = 16
PARTS = 3


def solution(mesh):
    rows = P(("dp", "expert"), None)
    experts = P("expert", None, None)
    grads = P("expert", "dp", None)
    return jax.shard_map(
        per_device,
        mesh=mesh,
        in_specs=(rows, rows, rows, rows, experts, experts, experts),
        out_specs=(rows, rows, rows, grads, grads, grads),
        check_vma=False,
    )
```

```python
import functools

import jax
import jax.numpy as jnp
from jax import lax
from jax.experimental import pallas as pl
from jax.experimental.pallas import tpu as pltpu
from jax.sharding import PartitionSpec as P

MESH = pl.DeviceIdType.MESH
F32 = jnp.float32
BF16 = jnp.bfloat16


def dot_nn(a, b):
    return lax.dot_general(a, b, (((1,), (0,)), ((), ())), preferred_element_type=F32)


def dot_nt(a, b):
    return lax.dot_general(a, b, (((1,), (1,)), ((), ())), preferred_element_type=F32)


def dot_tn(a, b):
    return lax.dot_general(a, b, (((0,), (0,)), ((), ())), preferred_element_type=F32)


def loop(count, body):
    def step(i, carry):
        body(i)
        return carry

    lax.fori_loop(0, count, step, 0)


def moe_kernel(
    owners, copies, base, rem, parts,
    ids_ref, probs_ref, tok_ref, ups_ref, wg_hbm, wu_hbm, wd_hbm,
    out_ref, gtok_ref, gprob_ref, ggate_ref, gup_ref, gdown_ref,
    wg, wu, wd, hot, hot_rem, back, back_rem,
    xs, cs, xr, cr, xe, ors, grs, rem_s, rem_r, xt, ct, xet,
    pre_g, pre_u, hid, gpre, gedge,
    sib_s, sib_r, z_s, z_in, tmp,
    w_sem, x_ss, x_rs, c_ss, c_rs, o_ss, o_rs, g_ss, g_rs, r_ss, r_rs,
    xe_ss, xe_rs, ge_ss, ge_rs, sib_ss, sib_rs, z_ss, z_rs,
):
    me = lax.axis_index("expert")
    dp = lax.axis_index("dp")
    levels = copies // 2
    core = lax.rem(dp, 2)
    z = dp // 2
    tok_count, width = tok_ref.shape
    ff = hid.shape[1]
    rows = width // copies
    chunk = 2 * rows
    main = owners * base
    slots_in = xr.shape[0]
    groups = PACK // rem if rem else 1
    group = width // groups
    ft = 256
    pw = ff // parts
    others = owners - 1
    sibling = {"dp": dp + 1 - 2 * core}
    right = {"dp": lax.rem(dp + 2, copies)}
    left = {"dp": lax.rem(dp + copies - 2, copies)}
    upper = z // (levels // 2)
    ahead = {"dp": lax.rem(dp + 2 - 4 * upper + copies, copies)}
    edge = z * (levels - 1 - z) == 0
    n_toward = upper * z + (1 - upper) * (levels - 1 - z)
    n_away = levels - 1 - n_toward

    def near_edge(body):
        if levels == 4:
            body()
        else:
            pl.when((z - 1) * (levels - 2 - z) == 0)(body)

    def far_from_edge(body):
        if levels > 4:
            pl.when((z - 1) * (levels - 2 - z) != 0)(body)

    w_copies = [
        pltpu.make_async_copy(src.at[0], dst, w_sem.at[i])
        for i, (src, dst) in enumerate(((wg_hbm, wg), (wu_hbm, wu), (wd_hbm, wd)))
    ]
    for copy in w_copies:
        copy.start()

    barrier = pltpu.get_barrier_semaphore()

    def greet(k):
        pl.semaphore_signal(
            barrier, inc=1, device_id={"expert": lax.rem(me + k + 1, owners)}, device_id_type=MESH
        )

    loop(others, greet)
    pl.semaphore_signal(barrier, inc=1, device_id=sibling, device_id_type=MESH)

    @pl.when(z > 0)
    def _():
        pl.semaphore_signal(barrier, inc=1, device_id=left, device_id_type=MESH)

    @pl.when(z < levels - 1)
    def _():
        pl.semaphore_signal(barrier, inc=1, device_id=right, device_id_type=MESH)

    ids = ids_ref[0:1, :]
    experts = lax.broadcasted_iota(jnp.int32, (max(owners, 8), tok_count), 0)
    match = (experts == ids).astype(BF16)
    before = (
        lax.broadcasted_iota(jnp.int32, (tok_count, tok_count), 0)
        < lax.broadcasted_iota(jnp.int32, (tok_count, tok_count), 1)
    ).astype(BF16)
    rank = jnp.sum(dot_nn(match, before) * match.astype(F32), axis=0, keepdims=True).astype(jnp.int32)
    target = jnp.where(rank < base, ids * base + rank, -1)
    hot[...] = (lax.broadcasted_iota(jnp.int32, (main, tok_count), 0) == target).astype(BF16)
    target_rem = jnp.where(rank < base, -PACK, ids * PACK + rank - base)
    if rem:
        slots = lax.broadcasted_iota(jnp.int32, (owners * PACK, tok_count), 0)
        for g in range(groups):
            hot_rem[g] = (slots == target_rem + g * rem).astype(BF16)

    def column(row):
        return jnp.transpose(jnp.broadcast_to(row, (8, tok_count)))[:, 0:1]


    def block(index):
        return pl.ds(pl.multiple_of(index * base, 16), base)

    def packed(index):
        return pl.ds(pl.multiple_of(index * PACK, 16), PACK)

    def level_at(s):
        return upper * s + (1 - upper) * (levels - 1 - s)

    def level_cols(level):
        return pl.ds(pl.multiple_of(level * chunk, 128), chunk)

    def block_copy(src, dst, ss, rs, s, k):
        peer = lax.rem(me + k + 1, owners)
        cols = level_cols(level_at(s))
        index = s * others + k
        return pltpu.make_async_remote_copy(
            src_ref=src.at[block(peer), cols],
            dst_ref=dst.at[block(me), cols],
            send_sem=ss.at[index],
            recv_sem=rs.at[index],
            device_id={"expert": peer},
            device_id_type=MESH,
        )

    def packed_copy(e, k):
        peer = lax.rem(me + k + 1, owners)
        return pltpu.make_async_remote_copy(
            src_ref=rem_s.at[e, packed(peer)],
            dst_ref=rem_r.at[e, packed(me)],
            send_sem=r_ss.at[e * others + k],
            recv_sem=r_rs.at[e * others + k],
            device_id={"expert": peer},
            device_id_type=MESH,
        )

    def send_packed(e, value):
        rem_s[e] = value.astype(BF16)
        loop(others, lambda k: packed_copy(e, k).start())
        rem_r[e, packed(me)] = rem_s[e, packed(me)]

    def dispatch_packed(e, values):
        if rem:
            send_packed(e, sum(
                dot_nn(hot_rem[g], values[:, g * group:(g + 1) * group]) for g in range(groups)
            ))

    def packed_match(g, shape, flat, wide):
        i = lax.broadcasted_iota(jnp.int32, shape, flat)
        j = lax.broadcasted_iota(jnp.int32, shape, wide)
        shift = rem.bit_length() - 1
        return (j == (i >> shift) * PACK + g * rem + (i & (rem - 1))).astype(BF16)

    def spread_packed(e, dst):
        if rem:
            loop(others, lambda k: packed_copy(e, k).wait_recv())
            arrived = rem_r[e]
            for g in range(groups):
                pick = packed_match(g, (owners * rem, owners * PACK), 0, 1)
                dst[main:main + owners * rem, g * group:(g + 1) * group] = dot_nn(pick, arrived).astype(BF16)

    def collect_packed(e, src):
        if rem:
            send_packed(e, sum(
                dot_nn(
                    packed_match(g, (owners * PACK, owners * rem), 1, 0),
                    src[main:main + owners * rem, g * group:(g + 1) * group],
                )
                for g in range(groups)
            ))

    def edge_x_copy(s, k):
        cols = level_cols(level_at(s))
        sender = block(lax.rem(me - k - 1 + owners, owners))
        return pltpu.make_async_remote_copy(
            src_ref=xr.at[sender, cols], dst_ref=xe.at[sender, cols],
            send_sem=xe_ss.at[s * owners + k], recv_sem=xe_rs.at[s * owners + k],
            device_id=ahead, device_id_type=MESH,
        )

    def edge_rem_copy():
        cols = pl.ds(pl.multiple_of((1 - upper) * chunk, 128), width - chunk)
        return pltpu.make_async_remote_copy(
            src_ref=xr.at[pl.ds(main, slots_in - main), cols], dst_ref=xe.at[pl.ds(main, slots_in - main), cols],
            send_sem=xe_ss.at[levels * owners], recv_sem=xe_rs.at[levels * owners],
            device_id=ahead, device_id_type=MESH,
        )

    def send_chunk(values, src, dst, ss, rs, s):
        cols = level_cols(level_at(s))
        src[0:main, cols] = dot_nn(hot[...], values[:, cols]).astype(BF16)
        loop(others, lambda k: block_copy(src, dst, ss, rs, s, k).start())
        dst[block(me), cols] = src[block(me), cols]

    beside = (z + levels - 1) // levels + (2 * levels - 2 - z) // levels
    pl.semaphore_wait(barrier, owners + beside)


    def send_tokens(s):
        send_chunk(tok_ref, xs, xr, x_ss, x_rs, s)

        @pl.when(jnp.logical_and(edge, s < levels - 1))
        def _():
            edge_x_copy(s, others).start()

    send_tokens(0)
    dispatch_packed(0, tok_ref)
    loop(levels - 1, lambda s: send_tokens(s + 1))
    probs = probs_ref[...]
    total = jnp.sum(probs, axis=0, keepdims=True)
    share_row = probs[0:1, :] / total

    share = column(share_row)
    gtok_ref[...] = (share * ups_ref[...].astype(F32)).astype(BF16)
    dispatch_packed(1, gtok_ref)

    place = lax.broadcasted_iota(jnp.int32, (tok_count, main), 1)
    back[...] = (place == column(target.astype(F32)).astype(jnp.int32)).astype(BF16)
    if rem:
        place = lax.broadcasted_iota(jnp.int32, (tok_count, owners * PACK), 1)
        target_col = column(target_rem.astype(F32)).astype(jnp.int32)
        for g in range(groups):
            back_rem[g] = (place == target_col + g * rem).astype(BF16)
    pre_g[...] = jnp.zeros_like(pre_g)
    pre_u[...] = jnp.zeros_like(pre_u)

    def part(p):
        return pl.ds(pl.multiple_of(p * pw, 128), pw)

    def edge_g_copy(p, i):
        return pltpu.make_async_remote_copy(
            src_ref=gpre.at[i, :, part(p)], dst_ref=gedge.at[i, :, part(p)],
            send_sem=ge_ss.at[p * 2 + i], recv_sem=ge_rs.at[p * 2 + i],
            device_id=ahead, device_id_type=MESH,
        )

    w_copies[0].wait()
    w_copies[1].wait()
    spread_packed(0, xr)
    if rem:
        @pl.when(edge)
        def _():
            edge_rem_copy().start()

    def arrive_x(s):
        def one(k):
            block_copy(xs, xr, x_ss, x_rs, s, k).wait_recv()

            @pl.when(jnp.logical_and(edge, s * owners + k <= (levels - 2) * owners))
            def _():
                edge_x_copy(s, k).start()

        loop(others, one)

        @pl.when(s > 0)
        def _():
            send_chunk(gtok_ref, cs, cr, c_ss, c_rs, s - 1)

    def flip(src, dst, s):
        level = level_at(s)
        dst[pl.ds(pl.multiple_of(level * chunk, 128), chunk), :] = jnp.transpose(src[:, level_cols(level)])

    def forward_chunk(s):
        arrive_x(s)
        depth = level_cols(level_at(s))

        def tile(j):
            cols = pl.ds(pl.multiple_of(j * ft, 128), ft)
            pre_g[:, cols] += dot_nn(xr[:, depth], wg[depth, cols])
            pre_u[:, cols] += dot_nn(xr[:, depth], wu[depth, cols])

        loop(ff // ft, tile)
        flip(xr, xt, s)

    loop(levels - 1, forward_chunk)
    arrive_x(levels - 1)
    send_chunk(gtok_ref, cs, cr, c_ss, c_rs, levels - 1)
    last = level_cols(level_at(levels - 1))

    def forward_last(j):
        cols = pl.ds(pl.multiple_of(j * ft, 128), ft)
        a = pre_g[:, cols] + dot_nn(xr[:, last], wg[last, cols])
        b = pre_u[:, cols] + dot_nn(xr[:, last], wu[last, cols])
        pre_g[:, cols] = a
        pre_u[:, cols] = b
        hid[:, cols] = (a * jax.nn.sigmoid(a) * b).astype(BF16)

    loop(ff // ft, forward_last)

    def own_rows(dest):
        return pl.ds(pl.multiple_of(dest * rows, 128), rows)

    def piece(m, dest, cols):
        if m == 0:
            return dot_nn(ct[own_rows(dest), :], hid[:, cols])
        return dot_nn(xt[own_rows(dest), :], gpre[m - 1, :, cols])

    def edge_piece(m, dest, cols):
        return dot_nn(xet[own_rows(dest), :], gedge[m - 1, :, cols])

    def full_piece(m, dest, cols):
        if levels == 4:
            return piece(m, dest, cols) + edge_piece(m, dest, cols)
        tmp[...] = piece(m, dest, cols)

        @near_edge
        def _():
            tmp[...] += edge_piece(m, dest, cols)

        return tmp[...]

    def sib_copy(slot, p=None):
        if p is None:
            src, dst, index = sib_s.at[slot], sib_r.at[slot], slot * parts
        else:
            src, dst, index = sib_s.at[slot, :, part(p)], sib_r.at[slot, :, part(p)], slot * parts + p
        return pltpu.make_async_remote_copy(
            src_ref=src, dst_ref=dst,
            send_sem=sib_ss.at[index], recv_sem=sib_rs.at[index],
            device_id=sibling, device_id_type=MESH,
        )

    slots_all = 3 * levels

    def landing(slot, way, level):
        spare = jnp.where(lax.rem(slot, levels) == level, slots_all + slot // levels, slot)
        return way * spare + (1 - way) * slot

    def line_copy(slot, p, way, level=None):
        index = landing(slot, way, z + 1 - 2 * way if level is None else level)
        return pltpu.make_async_remote_copy(
            src_ref=z_s.at[slot, :, part(p)], dst_ref=z_in.at[index, :, part(p)],
            send_sem=z_ss.at[slot * parts + p],
            recv_sem=z_rs.at[index * parts + p],
            device_id={"dp": lax.rem(dp + 2 - 4 * way + copies, copies)}, device_id_type=MESH,
        )

    def sib_whole(m, level):
        slot = m * levels + level

        def one(p):
            sib_s[slot, :, part(p)] = piece(m, level * 2 + 1 - core, part(p)).astype(BF16)

        loop(parts, one)
        sib_copy(slot).start()

    def sib_part(m, level, p):
        slot = m * levels + level
        dest = level * 2 + 1 - core
        sib_s[slot, :, part(p)] = full_piece(m, dest, part(p)).astype(BF16)
        sib_copy(slot, p).start()

    def add_line(slot, p, way):
        line_copy(slot, p, way, z).wait_recv()
        tmp[...] += z_in[landing(slot, way, z), :, part(p)].astype(F32)

    def push(slot, p, way):
        z_s[slot, :, part(p)] = tmp[...].astype(BF16)
        line_copy(slot, p, way).start()

    def level_of(s, way):
        return way * s + (1 - way) * (levels - 1 - s)

    def sib_wait(m, level):
        sib_copy(m * levels + level).wait_recv()

    def push_part(m, s, p, way, upstream):
        level = level_of(s, way)
        slot = m * levels + level
        tmp[...] = piece(m, level * 2 + core, part(p)) + sib_r[slot, :, part(p)].astype(F32)
        if upstream:
            add_line(slot, p, way)
        push(slot, p, way)

    def part_push(m, s, p):
        level = level_of(s, upper)
        slot = m * levels + level
        dest = level * 2 + core
        tmp[...] = full_piece(m, dest, part(p))

        @far_from_edge
        def _():
            add_line(slot, p, upper)

        sib_copy(slot, p).wait_recv()
        tmp[...] += sib_r[slot, :, part(p)].astype(F32)
        push(slot, p, upper)

    grads = (gdown_ref, ggate_ref, gup_ref)

    def own_sum(m):
        slot = m * levels + z
        sib_copy(slot).wait_recv()

        def one(p):
            grads[m][0, :, part(p)] = piece(m, z * 2 + core, part(p)) + sib_r[slot, :, part(p)].astype(F32)

        loop(parts, one)

    def own_part(m, p):
        slot = m * levels + z
        tmp[...] = full_piece(m, z * 2 + core, part(p))
        sib_copy(slot, p).wait_recv()
        grads[m][0, :, part(p)] = tmp[...] + sib_r[slot, :, part(p)].astype(F32)

    def finish_way(m, way):
        slot = m * levels + z

        def one(p):
            line_copy(slot, p, way, z).wait_recv()
            grads[m][0, :, part(p)] += z_in[landing(slot, way, z), :, part(p)].astype(F32)

        loop(parts, one)

    w_copies[2].wait()
    loop(levels, lambda s: loop(others, lambda k: block_copy(xs, xr, x_ss, x_rs, s, k).wait_send()))

    def out_tile(j):
        cols = pl.ds(pl.multiple_of(j * ft, 128), ft)
        xs[:, cols] = dot_nt(hid[...], wd[cols, :]).astype(BF16)

    flip(xr, xt, levels - 1)
    spread_packed(1, cr)

    def edge_flip(s):
        loop(owners, lambda k: edge_x_copy(s, k).wait_recv())
        flip(xe, xet, s)

    tiles = width // ft // levels

    def stage(s):
        loop(others, lambda k: block_copy(cs, cr, c_ss, c_rs, s, k).wait_recv())
        flip(cr, ct, s)
        sib_whole(0, level_at(s))

        if s < levels - 2:
            @pl.when(edge)
            def _():
                sib_wait(0, level_at(s))
                loop(parts, lambda p: push_part(0, s, p, upper, False))

        if 1 <= s <= 3:
            @pl.when(jnp.logical_not(edge))
            def _():
                if s == 1:
                    sib_wait(0, level_at(0))
                    push_part(0, 0, 0, upper, True)
                if s == 2:
                    loop(parts - 1, lambda p: push_part(0, 0, p + 1, upper, True))
                if s == 3:
                    sib_wait(0, level_at(1))
                    push_part(0, 1, 0, upper, True)

        loop(tiles, lambda j: out_tile(s * tiles + j))

    if rem:
        @pl.when(jnp.logical_not(edge))
        def _():
            near_edge(lambda: edge_rem_copy().wait_recv())

    for s in range(levels):
        stage(s)

    collect_packed(2, xs)
    loop(levels, lambda s: loop(others, lambda k: block_copy(xs, ors, o_ss, o_rs, s, k).start()))
    ors[block(me)] = xs[block(me)]

    def backward_tile(j):
        cols = pl.ds(pl.multiple_of(j * ft, 128), ft)
        grad = dot_nn(cr[...], wd[:, cols])
        a = pre_g[:, cols]
        s = jax.nn.sigmoid(a)
        gpre[0, :, cols] = (grad * pre_u[:, cols] * s * (1.0 + a * (1.0 - s))).astype(BF16)
        gpre[1, :, cols] = (grad * a * s).astype(BF16)

    loop(ff // ft, backward_tile)

    @pl.when(edge)
    def _():
        def one(p):
            edge_g_copy(p, 0).start()
            edge_g_copy(p, 1).start()

        loop(parts, one)

    loop(levels, lambda s: loop(others, lambda k: block_copy(cs, cr, c_ss, c_rs, s, k).wait_send()))

    def input_grad(s):
        def tile(j):
            cols = pl.ds(pl.multiple_of(level_at(s) * chunk + j * rows, 128), rows)
            cs[:, cols] = (dot_nt(gpre[0], wg[cols, :]) + dot_nt(gpre[1], wu[cols, :])).astype(BF16)

        loop(2, tile)
        loop(others, lambda k: block_copy(cs, grs, g_ss, g_rs, s, k).start())

    def input_grad_end():
        collect_packed(3, cs)
        grs[block(me)] = cs[block(me)]

    def tile_of(src, e, cols, g, offset):
        value = dot_nn(back[...], src[:, cols])
        if rem:
            value += dot_nn(back_rem[g], rem_r[e, :, offset:offset + ft])
        return value

    def take_out():
        if rem:
            loop(others, lambda k: packed_copy(2, k).wait_recv())
        loop(levels, lambda s: loop(others, lambda k: block_copy(xs, ors, o_ss, o_rs, s, k).wait_recv()))
        product = jnp.zeros((tok_count, 1), F32)
        for j in range(width // ft):
            cols = pl.ds(j * ft, ft)
            mixed = tile_of(ors, 2, cols, j * ft // group, j * ft % group)
            out_ref[:, cols] = (share * mixed).astype(BF16)
            product += jnp.sum(ups_ref[:, cols].astype(F32) * mixed, axis=1, keepdims=True)
        first = (lax.broadcasted_iota(jnp.int32, probs.shape, 0) == 0).astype(F32)
        product_row = jnp.transpose(jnp.broadcast_to(product, (tok_count, 128)))[0:1, :]
        gprob_ref[...] = (first - share_row) * (product_row / total)

    def take_input_grad():
        if rem:
            loop(others, lambda k: packed_copy(3, k).wait_recv())
        loop(levels, lambda s: loop(others, lambda k: block_copy(cs, grs, g_ss, g_rs, s, k).wait_recv()))
        for j in range(width // ft):
            cols = pl.ds(j * ft, ft)
            gtok_ref[:, cols] = tile_of(grs, 3, cols, j * ft // group, j * ft % group).astype(BF16)

    @pl.when(edge)
    def _():
        loop(others - 1, lambda k: edge_x_copy(levels - 2, k + 1).start())
        sib_wait(0, level_at(levels - 2))
        loop(parts, lambda p: push_part(0, levels - 2, p, upper, False))
        loop(levels, input_grad)
        input_grad_end()
        sib_whole(1, z)
        sib_whole(2, z)
        for m in range(3):
            own_sum(m)
        take_out()
        take_input_grad()
        for m in range(3):
            finish_way(m, 1 - upper)

    @pl.when(jnp.logical_not(edge))
    def _():
        loop(parts - 1, lambda p: push_part(0, 1, p + 1, upper, True))

        def later(s):
            @pl.when(s > 1)
            def _():
                sib_wait(0, level_at(s))
                loop(parts, lambda p: push_part(0, s, p, upper, True))

        if levels > 4:
            loop(n_toward, later)
        near_edge(lambda: loop(levels - 2, edge_flip))
        loop(levels // 2, input_grad)

        def toward_step(m, p):
            near_edge(lambda: edge_g_copy(p, m - 1).wait_recv())
            loop(n_toward, lambda s: sib_part(m, level_of(s, upper), p))
            loop(n_toward, lambda s: part_push(m, s, p))

        def away(s):
            level = level_of(s, 1 - upper)
            sib_whole(1, level)
            sib_whole(2, level)
            sib_wait(0, level)
            loop(parts, lambda p: push_part(0, s, p, 1 - upper, True))

        def away_step(m, p):
            def one(s):
                if p == 0:
                    sib_wait(m, level_of(s, 1 - upper))
                push_part(m, s, p, 1 - upper, True)

            loop(n_away, one)

        quarter = levels // 4
        steps = [(m, p) for p in range(parts) for m in (1, 2)]
        for i, (m, p) in enumerate(steps):
            toward_step(m, p)
            if i < 2:
                loop(quarter, lambda s: input_grad(levels // 2 + i * quarter + s))
            if i == 1:
                input_grad_end()
            if i == 2:
                loop(n_away, away)
                own_sum(0)
                away_step(*steps[0])
                away_step(*steps[1])
            if i == 3:
                take_out()
            if i > 2:
                away_step(*steps[i - 1])
        near_edge(lambda: edge_flip(levels - 2))
        for m in (1, 2):
            loop(parts, lambda p: sib_part(m, z, p))
        for m in (1, 2):
            loop(parts, lambda p: own_part(m, p))
        take_input_grad()
        away_step(*steps[-1])
        finish_way(0, 1 - upper)

        @far_from_edge
        def _():
            finish_way(1, upper)
            finish_way(2, upper)

        finish_way(1, 1 - upper)
        finish_way(2, 1 - upper)
        finish_way(0, upper)

    loop(levels, lambda s: loop(others, lambda k: block_copy(xs, ors, o_ss, o_rs, s, k).wait_send()))
    loop(levels, lambda s: loop(others, lambda k: block_copy(cs, grs, g_ss, g_rs, s, k).wait_send()))
    if rem:
        loop(4, lambda e: loop(others, lambda k: packed_copy(e, k).wait_send()))
    loop(levels, lambda slot: sib_copy(slot).wait_send())

    def sent(m, level):
        @pl.when(level != z)
        def _():
            loop(parts, lambda p: line_copy(m * levels + level, p, 0).wait_send())

    loop(levels, lambda level: sent(0, level))

    @pl.when(edge)
    def _():
        sib_copy(levels + z).wait_send()
        sib_copy(2 * levels + z).wait_send()
        loop(levels - 1, lambda s: loop(owners, lambda k: edge_x_copy(s, k).wait_send()))
        loop(parts, lambda p: edge_g_copy(p, 0).wait_send())
        loop(parts, lambda p: edge_g_copy(p, 1).wait_send())
        if rem:
            edge_rem_copy().wait_send()

    @pl.when(jnp.logical_not(edge))
    def _():
        for m in (1, 2):
            loop(levels, lambda level: sent(m, level))
            loop(n_away, lambda s: sib_copy(m * levels + level_of(s, 1 - upper)).wait_send())
            loop(n_toward + 1, lambda s: loop(
                parts, lambda p: sib_copy(m * levels + level_of(s, upper), p).wait_send()
            ))


def copy_kernel(*refs):
    sems = refs[18]
    reads = [pltpu.make_async_copy(refs[i], refs[12 + i], sems.at[i]) for i in range(6)]
    writes = [pltpu.make_async_copy(refs[12 + i], refs[6 + i], sems.at[6 + i]) for i in range(6)]
    for move in reads:
        move.start()
    for read, write in zip(reads, writes):
        read.wait()
        write.start()
    for move in writes:
        move.wait()


def per_device(tokens, expert_ids, gate_probs, upstream, w_gate, w_up, w_down):
    tok_count, width = tokens.shape
    owners = lax.axis_size("expert")
    copies = lax.axis_size("dp")
    ff = w_gate.shape[2]
    capacity = tok_count // owners * 5 // 2
    rem = capacity % 16
    if rem == 0 or PACK % rem or (owners * rem) % 16:
        rem = 0
    base = capacity - rem if rem else -(-capacity // 16) * 16
    main = owners * base
    slots = main + owners * rem
    groups = PACK // rem if rem else 1
    levels = copies // 2
    rows = width // copies
    parts = PARTS
    others = owners - 1
    vmem = pl.BlockSpec(memory_space=pltpu.VMEM)
    hbm = pl.BlockSpec(memory_space=pl.ANY)
    dma = pltpu.SemaphoreType.DMA
    weight = pltpu.VMEM((width, ff), BF16)
    wide = pltpu.VMEM((slots, width), BF16)
    back = pltpu.VMEM((main, width), BF16)
    turned = pltpu.VMEM((width, slots), BF16)
    narrow = pltpu.VMEM((slots, ff), BF16)
    stack = pltpu.VMEM((3 * levels, rows, ff), BF16)
    packed = pltpu.VMEM((4, owners * PACK, width // groups), BF16)
    grad = jax.ShapeDtypeStruct((1, rows, ff), F32)
    results = pl.pallas_call(
        functools.partial(moe_kernel, owners, copies, base, rem, parts),
        out_shape=(
            jax.ShapeDtypeStruct((tok_count, width), BF16),
            jax.ShapeDtypeStruct((tok_count, width), BF16),
            jax.ShapeDtypeStruct(gate_probs.shape[::-1], F32),
            grad, grad, grad,
        ),
        in_specs=[vmem, vmem, vmem, vmem, hbm, hbm, hbm],
        out_specs=(vmem,) * 6,
        scratch_shapes=[
            weight, weight, weight,
            pltpu.VMEM((main, tok_count), BF16),
            pltpu.VMEM((groups, owners * PACK, tok_count), BF16),
            pltpu.VMEM((tok_count, main), BF16),
            pltpu.VMEM((groups, tok_count, owners * PACK), BF16),
            wide, wide, wide, wide, wide, back, back,
            packed, packed,
            turned, turned, turned,
            pltpu.VMEM((slots, ff), F32), pltpu.VMEM((slots, ff), F32),
            narrow, pltpu.VMEM((2, slots, ff), BF16), pltpu.VMEM((2, slots, ff), BF16),
            stack, stack, stack,
            pltpu.VMEM((3 * levels + 3, rows, ff), BF16),
            pltpu.VMEM((rows, ff // parts), F32),
            dma((3,)),
            *[dma((levels * others,))] * 8,
            dma((4 * others,)), dma((4 * others,)),
            dma((levels * owners + 1,)), dma((levels * owners + 1,)),
            dma((2 * parts,)), dma((2 * parts,)),
            *[dma((3 * levels * parts,))] * 3,
            dma(((3 * levels + 3) * parts,)),
        ],
        compiler_params=pltpu.CompilerParams(
            collective_id=0, has_side_effects=True, vmem_limit_bytes=62 * 2**20
        ),
    )(expert_ids.T, gate_probs.T, tokens, upstream, w_gate, w_up, w_down)
    layer_out, grad_tokens, grad_probs, grad_gate, grad_up, grad_down = pl.pallas_call(
        copy_kernel,
        out_shape=[jax.ShapeDtypeStruct(r.shape, r.dtype) for r in results],
        in_specs=[hbm] * 6,
        out_specs=[hbm] * 6,
        scratch_shapes=[pltpu.VMEM(r.shape, r.dtype) for r in results] + [dma((12,))],
    )(*results)
    return (layer_out, grad_tokens, grad_probs.T, grad_gate, grad_up, grad_down)


PACK = 16
PARTS = 3


def solution(mesh):
    rows = P(("dp", "expert"), None)
    experts = P("expert", None, None)
    grads = P("expert", "dp", None)
    return jax.shard_map(
        per_device,
        mesh=mesh,
        in_specs=(rows, rows, rows, rows, experts, experts, experts),
        out_specs=(rows, rows, rows, grads, grads, grads),
        check_vma=False,
    )
```

```python
import functools

import jax
import jax.numpy as jnp
from jax import lax
from jax.experimental import pallas as pl
from jax.experimental.pallas import tpu as pltpu
from jax.sharding import PartitionSpec as P

MESH = pl.DeviceIdType.MESH
F32 = jnp.float32
BF16 = jnp.bfloat16


def dot_nn(a, b):
    return lax.dot_general(a, b, (((1,), (0,)), ((), ())), preferred_element_type=F32)


def dot_nt(a, b):
    return lax.dot_general(a, b, (((1,), (1,)), ((), ())), preferred_element_type=F32)


def dot_tn(a, b):
    return lax.dot_general(a, b, (((0,), (0,)), ((), ())), preferred_element_type=F32)


def loop(count, body):
    def step(i, carry):
        body(i)
        return carry

    lax.fori_loop(0, count, step, 0)


def moe_kernel(
    owners, copies, base, rem, parts,
    ids_ref, probs_ref, tok_ref, ups_ref, wg_hbm, wu_hbm, wd_hbm,
    out_ref, gtok_ref, gprob_ref, ggate_ref, gup_ref, gdown_ref,
    wg, wu, wd, hot, hot_rem, back, back_rem,
    xs, cs, xr, cr, xe, ors, grs, rem_s, rem_r, xt, ct, xet,
    pre_g, pre_u, hid, gpre, gedge,
    sib_s, sib_r, z_s, z_in, tmp,
    w_sem, x_ss, x_rs, c_ss, c_rs, o_ss, o_rs, g_ss, g_rs, r_ss, r_rs,
    xe_ss, xe_rs, ge_ss, ge_rs, sib_ss, sib_rs, z_ss, z_rs,
):
    me = lax.axis_index("expert")
    dp = lax.axis_index("dp")
    levels = copies // 2
    core = lax.rem(dp, 2)
    z = dp // 2
    tok_count, width = tok_ref.shape
    ff = hid.shape[1]
    rows = width // copies
    chunk = 2 * rows
    main = owners * base
    slots_in = xr.shape[0]
    groups = PACK // rem if rem else 1
    group = width // groups
    ft = 256
    pw = ff // parts
    others = owners - 1
    sibling = {"dp": dp + 1 - 2 * core}
    right = {"dp": lax.rem(dp + 2, copies)}
    left = {"dp": lax.rem(dp + copies - 2, copies)}
    upper = z // (levels // 2)
    ahead = {"dp": lax.rem(dp + 2 - 4 * upper + copies, copies)}
    edge = z * (levels - 1 - z) == 0
    n_toward = upper * z + (1 - upper) * (levels - 1 - z)
    n_away = levels - 1 - n_toward

    def near_edge(body):
        if levels == 4:
            body()
        else:
            pl.when((z - 1) * (levels - 2 - z) == 0)(body)

    def far_from_edge(body):
        if levels > 4:
            pl.when((z - 1) * (levels - 2 - z) != 0)(body)

    w_copies = [
        pltpu.make_async_copy(src.at[0], dst, w_sem.at[i])
        for i, (src, dst) in enumerate(((wg_hbm, wg), (wu_hbm, wu), (wd_hbm, wd)))
    ]
    for copy in w_copies:
        copy.start()

    barrier = pltpu.get_barrier_semaphore()

    def greet(k):
        pl.semaphore_signal(
            barrier, inc=1, device_id={"expert": lax.rem(me + k + 1, owners)}, device_id_type=MESH
        )

    loop(others, greet)
    pl.semaphore_signal(barrier, inc=1, device_id=sibling, device_id_type=MESH)

    @pl.when(z > 0)
    def _():
        pl.semaphore_signal(barrier, inc=1, device_id=left, device_id_type=MESH)

    @pl.when(z < levels - 1)
    def _():
        pl.semaphore_signal(barrier, inc=1, device_id=right, device_id_type=MESH)

    ids = ids_ref[0:1, :]
    experts = lax.broadcasted_iota(jnp.int32, (max(owners, 8), tok_count), 0)
    match = (experts == ids).astype(BF16)
    before = (
        lax.broadcasted_iota(jnp.int32, (tok_count, tok_count), 0)
        < lax.broadcasted_iota(jnp.int32, (tok_count, tok_count), 1)
    ).astype(BF16)
    rank = jnp.sum(dot_nn(match, before) * match.astype(F32), axis=0, keepdims=True).astype(jnp.int32)
    target = jnp.where(rank < base, ids * base + rank, -1)
    hot[...] = (lax.broadcasted_iota(jnp.int32, (main, tok_count), 0) == target).astype(BF16)
    target_rem = jnp.where(rank < base, -PACK, ids * PACK + rank - base)
    if rem:
        slots = lax.broadcasted_iota(jnp.int32, (owners * PACK, tok_count), 0)
        for g in range(groups):
            hot_rem[g] = (slots == target_rem + g * rem).astype(BF16)

    def column(row):
        return jnp.transpose(jnp.broadcast_to(row, (8, tok_count)))[:, 0:1]


    def block(index):
        return pl.ds(pl.multiple_of(index * base, 16), base)

    def packed(index):
        return pl.ds(pl.multiple_of(index * PACK, 16), PACK)

    def level_at(s):
        return upper * s + (1 - upper) * (levels - 1 - s)

    def level_cols(level):
        return pl.ds(pl.multiple_of(level * chunk, 128), chunk)

    def block_copy(src, dst, ss, rs, s, k):
        peer = lax.rem(me + k + 1, owners)
        cols = level_cols(level_at(s))
        index = s * others + k
        return pltpu.make_async_remote_copy(
            src_ref=src.at[block(peer), cols],
            dst_ref=dst.at[block(me), cols],
            send_sem=ss.at[index],
            recv_sem=rs.at[index],
            device_id={"expert": peer},
            device_id_type=MESH,
        )

    def packed_copy(e, k):
        peer = lax.rem(me + k + 1, owners)
        return pltpu.make_async_remote_copy(
            src_ref=rem_s.at[e, packed(peer)],
            dst_ref=rem_r.at[e, packed(me)],
            send_sem=r_ss.at[e * others + k],
            recv_sem=r_rs.at[e * others + k],
            device_id={"expert": peer},
            device_id_type=MESH,
        )

    def send_packed(e, value):
        rem_s[e] = value.astype(BF16)
        loop(others, lambda k: packed_copy(e, k).start())
        rem_r[e, packed(me)] = rem_s[e, packed(me)]

    def dispatch_packed(e, values):
        if rem:
            send_packed(e, sum(
                dot_nn(hot_rem[g], values[:, g * group:(g + 1) * group]) for g in range(groups)
            ))

    def packed_match(g, shape, flat, wide):
        i = lax.broadcasted_iota(jnp.int32, shape, flat)
        j = lax.broadcasted_iota(jnp.int32, shape, wide)
        shift = rem.bit_length() - 1
        return (j == (i >> shift) * PACK + g * rem + (i & (rem - 1))).astype(BF16)

    def spread_packed(e, dst):
        if rem:
            loop(others, lambda k: packed_copy(e, k).wait_recv())
            arrived = rem_r[e]
            for g in range(groups):
                pick = packed_match(g, (owners * rem, owners * PACK), 0, 1)
                dst[main:main + owners * rem, g * group:(g + 1) * group] = dot_nn(pick, arrived).astype(BF16)

    def collect_packed(e, src):
        if rem:
            send_packed(e, sum(
                dot_nn(
                    packed_match(g, (owners * PACK, owners * rem), 1, 0),
                    src[main:main + owners * rem, g * group:(g + 1) * group],
                )
                for g in range(groups)
            ))

    def edge_x_copy(s, k):
        cols = level_cols(level_at(s))
        sender = block(lax.rem(me - k - 1 + owners, owners))
        return pltpu.make_async_remote_copy(
            src_ref=xr.at[sender, cols], dst_ref=xe.at[sender, cols],
            send_sem=xe_ss.at[s * owners + k], recv_sem=xe_rs.at[s * owners + k],
            device_id=ahead, device_id_type=MESH,
        )

    def edge_rem_copy():
        cols = pl.ds(pl.multiple_of((1 - upper) * chunk, 128), width - chunk)
        return pltpu.make_async_remote_copy(
            src_ref=xr.at[pl.ds(main, slots_in - main), cols], dst_ref=xe.at[pl.ds(main, slots_in - main), cols],
            send_sem=xe_ss.at[levels * owners], recv_sem=xe_rs.at[levels * owners],
            device_id=ahead, device_id_type=MESH,
        )

    def send_chunk(values, src, dst, ss, rs, s):
        cols = level_cols(level_at(s))
        src[0:main, cols] = dot_nn(hot[...], values[:, cols]).astype(BF16)
        loop(others, lambda k: block_copy(src, dst, ss, rs, s, k).start())
        dst[block(me), cols] = src[block(me), cols]

    beside = (z + levels - 1) // levels + (2 * levels - 2 - z) // levels
    pl.semaphore_wait(barrier, owners + beside)


    def send_tokens(s):
        send_chunk(tok_ref, xs, xr, x_ss, x_rs, s)

        @pl.when(jnp.logical_and(edge, s < levels - 1))
        def _():
            edge_x_copy(s, others).start()

    send_tokens(0)
    dispatch_packed(0, tok_ref)
    loop(levels - 1, lambda s: send_tokens(s + 1))
    probs = probs_ref[...]
    total = jnp.sum(probs, axis=0, keepdims=True)
    share_row = probs[0:1, :] / total

    share = column(share_row)
    gtok_ref[...] = (share * ups_ref[...].astype(F32)).astype(BF16)
    dispatch_packed(1, gtok_ref)

    place = lax.broadcasted_iota(jnp.int32, (tok_count, main), 1)
    back[...] = (place == column(target.astype(F32)).astype(jnp.int32)).astype(BF16)
    if rem:
        place = lax.broadcasted_iota(jnp.int32, (tok_count, owners * PACK), 1)
        target_col = column(target_rem.astype(F32)).astype(jnp.int32)
        for g in range(groups):
            back_rem[g] = (place == target_col + g * rem).astype(BF16)
    pre_g[...] = jnp.zeros_like(pre_g)
    pre_u[...] = jnp.zeros_like(pre_u)

    def part(p):
        return pl.ds(pl.multiple_of(p * pw, 128), pw)

    def edge_g_copy(p, i):
        return pltpu.make_async_remote_copy(
            src_ref=gpre.at[i, :, part(p)], dst_ref=gedge.at[i, :, part(p)],
            send_sem=ge_ss.at[p * 2 + i], recv_sem=ge_rs.at[p * 2 + i],
            device_id=ahead, device_id_type=MESH,
        )

    w_copies[0].wait()
    w_copies[1].wait()
    spread_packed(0, xr)
    if rem:
        @pl.when(edge)
        def _():
            edge_rem_copy().start()

    def arrive_x(s):
        def one(k):
            block_copy(xs, xr, x_ss, x_rs, s, k).wait_recv()

            @pl.when(jnp.logical_and(edge, s * owners + k <= (levels - 2) * owners))
            def _():
                edge_x_copy(s, k).start()

        loop(others, one)

        @pl.when(s > 0)
        def _():
            send_chunk(gtok_ref, cs, cr, c_ss, c_rs, s - 1)

    def flip(src, dst, s):
        level = level_at(s)
        dst[pl.ds(pl.multiple_of(level * chunk, 128), chunk), :] = jnp.transpose(src[:, level_cols(level)])

    def forward_chunk(s):
        arrive_x(s)
        depth = level_cols(level_at(s))

        def tile(j):
            cols = pl.ds(pl.multiple_of(j * ft, 128), ft)
            pre_g[:, cols] += dot_nn(xr[:, depth], wg[depth, cols])
            pre_u[:, cols] += dot_nn(xr[:, depth], wu[depth, cols])

        loop(ff // ft, tile)
        flip(xr, xt, s)

    loop(levels - 1, forward_chunk)
    arrive_x(levels - 1)
    send_chunk(gtok_ref, cs, cr, c_ss, c_rs, levels - 1)
    last = level_cols(level_at(levels - 1))

    def forward_last(j):
        cols = pl.ds(pl.multiple_of(j * ft, 128), ft)
        a = pre_g[:, cols] + dot_nn(xr[:, last], wg[last, cols])
        b = pre_u[:, cols] + dot_nn(xr[:, last], wu[last, cols])
        pre_g[:, cols] = a
        pre_u[:, cols] = b
        hid[:, cols] = (a * jax.nn.sigmoid(a) * b).astype(BF16)

    loop(ff // ft, forward_last)

    def own_rows(dest):
        return pl.ds(pl.multiple_of(dest * rows, 128), rows)

    def piece(m, dest, cols):
        if m == 0:
            return dot_nn(ct[own_rows(dest), :], hid[:, cols])
        return dot_nn(xt[own_rows(dest), :], gpre[m - 1, :, cols])

    def edge_piece(m, dest, cols):
        return dot_nn(xet[own_rows(dest), :], gedge[m - 1, :, cols])

    def full_piece(m, dest, cols):
        if levels == 4:
            return piece(m, dest, cols) + edge_piece(m, dest, cols)
        tmp[...] = piece(m, dest, cols)

        @near_edge
        def _():
            tmp[...] += edge_piece(m, dest, cols)

        return tmp[...]

    def sib_copy(slot, p=None):
        if p is None:
            src, dst, index = sib_s.at[slot], sib_r.at[slot], slot * parts
        else:
            src, dst, index = sib_s.at[slot, :, part(p)], sib_r.at[slot, :, part(p)], slot * parts + p
        return pltpu.make_async_remote_copy(
            src_ref=src, dst_ref=dst,
            send_sem=sib_ss.at[index], recv_sem=sib_rs.at[index],
            device_id=sibling, device_id_type=MESH,
        )

    slots_all = 3 * levels

    def landing(slot, way, level):
        spare = jnp.where(lax.rem(slot, levels) == level, slots_all + slot // levels, slot)
        return way * spare + (1 - way) * slot

    def line_copy(slot, p, way, level=None):
        index = landing(slot, way, z + 1 - 2 * way if level is None else level)
        return pltpu.make_async_remote_copy(
            src_ref=z_s.at[slot, :, part(p)], dst_ref=z_in.at[index, :, part(p)],
            send_sem=z_ss.at[slot * parts + p],
            recv_sem=z_rs.at[index * parts + p],
            device_id={"dp": lax.rem(dp + 2 - 4 * way + copies, copies)}, device_id_type=MESH,
        )

    def sib_whole(m, level):
        slot = m * levels + level

        def one(p):
            sib_s[slot, :, part(p)] = piece(m, level * 2 + 1 - core, part(p)).astype(BF16)

        loop(parts, one)
        sib_copy(slot).start()

    def sib_part(m, level, p):
        slot = m * levels + level
        dest = level * 2 + 1 - core
        sib_s[slot, :, part(p)] = full_piece(m, dest, part(p)).astype(BF16)
        sib_copy(slot, p).start()

    def add_line(slot, p, way):
        line_copy(slot, p, way, z).wait_recv()
        tmp[...] += z_in[landing(slot, way, z), :, part(p)].astype(F32)

    def push(slot, p, way):
        z_s[slot, :, part(p)] = tmp[...].astype(BF16)
        line_copy(slot, p, way).start()

    def level_of(s, way):
        return way * s + (1 - way) * (levels - 1 - s)

    def sib_wait(m, level):
        sib_copy(m * levels + level).wait_recv()

    def push_part(m, s, p, way, upstream):
        level = level_of(s, way)
        slot = m * levels + level
        tmp[...] = piece(m, level * 2 + core, part(p)) + sib_r[slot, :, part(p)].astype(F32)
        if upstream:
            add_line(slot, p, way)
        push(slot, p, way)

    def part_push(m, s, p):
        level = level_of(s, upper)
        slot = m * levels + level
        dest = level * 2 + core
        tmp[...] = full_piece(m, dest, part(p))

        @far_from_edge
        def _():
            add_line(slot, p, upper)

        sib_copy(slot, p).wait_recv()
        tmp[...] += sib_r[slot, :, part(p)].astype(F32)
        push(slot, p, upper)

    grads = (gdown_ref, ggate_ref, gup_ref)

    def own_sum(m):
        slot = m * levels + z
        sib_copy(slot).wait_recv()

        def one(p):
            grads[m][0, :, part(p)] = piece(m, z * 2 + core, part(p)) + sib_r[slot, :, part(p)].astype(F32)

        loop(parts, one)

    def own_part(m, p):
        slot = m * levels + z
        tmp[...] = full_piece(m, z * 2 + core, part(p))
        sib_copy(slot, p).wait_recv()
        grads[m][0, :, part(p)] = tmp[...] + sib_r[slot, :, part(p)].astype(F32)

    def finish_way(m, way):
        slot = m * levels + z

        def one(p):
            line_copy(slot, p, way, z).wait_recv()
            grads[m][0, :, part(p)] += z_in[landing(slot, way, z), :, part(p)].astype(F32)

        loop(parts, one)

    w_copies[2].wait()
    loop(levels, lambda s: loop(others, lambda k: block_copy(xs, xr, x_ss, x_rs, s, k).wait_send()))

    def out_tile(j):
        cols = pl.ds(pl.multiple_of(j * ft, 128), ft)
        xs[:, cols] = dot_nt(hid[...], wd[cols, :]).astype(BF16)

    flip(xr, xt, levels - 1)
    spread_packed(1, cr)

    def edge_flip(s):
        loop(owners, lambda k: edge_x_copy(s, k).wait_recv())
        flip(xe, xet, s)

    tiles = width // ft // levels

    def stage(s):
        loop(others, lambda k: block_copy(cs, cr, c_ss, c_rs, s, k).wait_recv())
        flip(cr, ct, s)
        sib_whole(0, level_at(s))

        if s < levels - 2:
            @pl.when(edge)
            def _():
                sib_wait(0, level_at(s))
                loop(parts, lambda p: push_part(0, s, p, upper, False))

        if 1 <= s <= 3:
            @pl.when(jnp.logical_not(edge))
            def _():
                if s == 1:
                    sib_wait(0, level_at(0))
                    push_part(0, 0, 0, upper, True)
                if s == 2:
                    loop(parts - 1, lambda p: push_part(0, 0, p + 1, upper, True))
                if s == 3:
                    sib_wait(0, level_at(1))
                    push_part(0, 1, 0, upper, True)

        loop(tiles, lambda j: out_tile(s * tiles + j))

    if rem:
        @pl.when(jnp.logical_not(edge))
        def _():
            near_edge(lambda: edge_rem_copy().wait_recv())

    for s in range(levels):
        stage(s)

    collect_packed(2, xs)
    loop(levels, lambda s: loop(others, lambda k: block_copy(xs, ors, o_ss, o_rs, s, k).start()))
    ors[block(me)] = xs[block(me)]

    def backward_tile(j):
        cols = pl.ds(pl.multiple_of(j * ft, 128), ft)
        grad = dot_nn(cr[...], wd[:, cols])
        a = pre_g[:, cols]
        s = jax.nn.sigmoid(a)
        gpre[0, :, cols] = (grad * pre_u[:, cols] * s * (1.0 + a * (1.0 - s))).astype(BF16)
        gpre[1, :, cols] = (grad * a * s).astype(BF16)

    loop(ff // ft, backward_tile)

    @pl.when(edge)
    def _():
        def one(p):
            edge_g_copy(p, 0).start()
            edge_g_copy(p, 1).start()

        loop(parts, one)

    loop(levels, lambda s: loop(others, lambda k: block_copy(cs, cr, c_ss, c_rs, s, k).wait_send()))

    def input_grad(s):
        def tile(j):
            cols = pl.ds(pl.multiple_of(level_at(s) * chunk + j * rows, 128), rows)
            cs[:, cols] = (dot_nt(gpre[0], wg[cols, :]) + dot_nt(gpre[1], wu[cols, :])).astype(BF16)

        loop(2, tile)
        loop(others, lambda k: block_copy(cs, grs, g_ss, g_rs, s, k).start())

    def input_grad_end():
        collect_packed(3, cs)
        grs[block(me)] = cs[block(me)]

    def tile_of(src, e, cols, g, offset):
        value = dot_nn(back[...], src[:, cols])
        if rem:
            value += dot_nn(back_rem[g], rem_r[e, :, offset:offset + ft])
        return value

    def take_out():
        if rem:
            loop(others, lambda k: packed_copy(2, k).wait_recv())
        loop(levels, lambda s: loop(others, lambda k: block_copy(xs, ors, o_ss, o_rs, s, k).wait_recv()))
        product = jnp.zeros((tok_count, 1), F32)
        for j in range(width // ft):
            cols = pl.ds(j * ft, ft)
            mixed = tile_of(ors, 2, cols, j * ft // group, j * ft % group)
            out_ref[:, cols] = (share * mixed).astype(BF16)
            product += jnp.sum(ups_ref[:, cols].astype(F32) * mixed, axis=1, keepdims=True)
        first = (lax.broadcasted_iota(jnp.int32, probs.shape, 0) == 0).astype(F32)
        product_row = jnp.transpose(jnp.broadcast_to(product, (tok_count, 128)))[0:1, :]
        gprob_ref[...] = (first - share_row) * (product_row / total)

    def take_input_grad():
        if rem:
            loop(others, lambda k: packed_copy(3, k).wait_recv())
        loop(levels, lambda s: loop(others, lambda k: block_copy(cs, grs, g_ss, g_rs, s, k).wait_recv()))
        for j in range(width // ft):
            cols = pl.ds(j * ft, ft)
            gtok_ref[:, cols] = tile_of(grs, 3, cols, j * ft // group, j * ft % group).astype(BF16)

    @pl.when(edge)
    def _():
        loop(others - 1, lambda k: edge_x_copy(levels - 2, k + 1).start())
        sib_wait(0, level_at(levels - 2))
        loop(parts, lambda p: push_part(0, levels - 2, p, upper, False))
        loop(levels, input_grad)
        input_grad_end()
        sib_whole(1, z)
        sib_whole(2, z)
        for m in range(3):
            own_sum(m)
        take_out()
        take_input_grad()
        for m in range(3):
            finish_way(m, 1 - upper)

    @pl.when(jnp.logical_not(edge))
    def _():
        loop(parts - 1, lambda p: push_part(0, 1, p + 1, upper, True))

        def later(s):
            @pl.when(s > 1)
            def _():
                sib_wait(0, level_at(s))
                loop(parts, lambda p: push_part(0, s, p, upper, True))

        if levels > 4:
            loop(n_toward, later)
        near_edge(lambda: loop(levels - 2, edge_flip))
        loop(levels // 2, input_grad)

        def near_push(m, p):
            loop(n_toward - 1, lambda s: part_push(m, s + 1, p))

        def toward_step(m, p):
            near_edge(lambda: edge_g_copy(p, m - 1).wait_recv())
            loop(n_toward, lambda s: sib_part(m, level_of(s, upper), p))
            part_push(m, 0, p)

        def away(s):
            level = level_of(s, 1 - upper)
            sib_whole(1, level)
            sib_whole(2, level)
            sib_wait(0, level)
            loop(parts, lambda p: push_part(0, s, p, 1 - upper, True))

        def away_step(m, p):
            def one(s):
                if p == 0:
                    sib_wait(m, level_of(s, 1 - upper))
                push_part(m, s, p, 1 - upper, True)

            loop(n_away, one)

        quarter = levels // 4
        steps = [(m, p) for p in range(parts) for m in (1, 2)]
        for i, (m, p) in enumerate(steps):
            toward_step(m, p)
            if i < 3:
                near_push(m, p)
            if i < 2:
                loop(quarter, lambda s: input_grad(levels // 2 + i * quarter + s))
            if i == 1:
                input_grad_end()
            if i == 2:
                loop(n_away, away)
                own_sum(0)
                away_step(*steps[0])
            if i == 3:
                take_out()
                away_step(*steps[1])
            if i > 3:
                away_step(*steps[i - 2])
        for m, p in steps[3:]:
            near_push(m, p)
        away_step(*steps[-2])
        near_edge(lambda: edge_flip(levels - 2))
        for m in (1, 2):
            loop(parts, lambda p: sib_part(m, z, p))
        for m in (1, 2):
            loop(parts, lambda p: own_part(m, p))
        away_step(*steps[-1])
        take_input_grad()
        finish_way(0, 1 - upper)

        @far_from_edge
        def _():
            finish_way(1, upper)
            finish_way(2, upper)

        finish_way(1, 1 - upper)
        finish_way(2, 1 - upper)
        finish_way(0, upper)

    loop(levels, lambda s: loop(others, lambda k: block_copy(xs, ors, o_ss, o_rs, s, k).wait_send()))
    loop(levels, lambda s: loop(others, lambda k: block_copy(cs, grs, g_ss, g_rs, s, k).wait_send()))
    if rem:
        loop(4, lambda e: loop(others, lambda k: packed_copy(e, k).wait_send()))
    loop(levels, lambda slot: sib_copy(slot).wait_send())

    def sent(m, level):
        @pl.when(level != z)
        def _():
            loop(parts, lambda p: line_copy(m * levels + level, p, 0).wait_send())

    loop(levels, lambda level: sent(0, level))

    @pl.when(edge)
    def _():
        sib_copy(levels + z).wait_send()
        sib_copy(2 * levels + z).wait_send()
        loop(levels - 1, lambda s: loop(owners, lambda k: edge_x_copy(s, k).wait_send()))
        loop(parts, lambda p: edge_g_copy(p, 0).wait_send())
        loop(parts, lambda p: edge_g_copy(p, 1).wait_send())
        if rem:
            edge_rem_copy().wait_send()

    @pl.when(jnp.logical_not(edge))
    def _():
        for m in (1, 2):
            loop(levels, lambda level: sent(m, level))
            loop(n_away, lambda s: sib_copy(m * levels + level_of(s, 1 - upper)).wait_send())
            loop(n_toward + 1, lambda s: loop(
                parts, lambda p: sib_copy(m * levels + level_of(s, upper), p).wait_send()
            ))


def copy_kernel(*refs):
    sems = refs[18]
    reads = [pltpu.make_async_copy(refs[i], refs[12 + i], sems.at[i]) for i in range(6)]
    writes = [pltpu.make_async_copy(refs[12 + i], refs[6 + i], sems.at[6 + i]) for i in range(6)]
    for move in reads:
        move.start()
    for read, write in zip(reads, writes):
        read.wait()
        write.start()
    for move in writes:
        move.wait()


def per_device(tokens, expert_ids, gate_probs, upstream, w_gate, w_up, w_down):
    tok_count, width = tokens.shape
    owners = lax.axis_size("expert")
    copies = lax.axis_size("dp")
    ff = w_gate.shape[2]
    capacity = tok_count // owners * 5 // 2
    rem = capacity % 16
    if rem == 0 or PACK % rem or (owners * rem) % 16:
        rem = 0
    base = capacity - rem if rem else -(-capacity // 16) * 16
    main = owners * base
    slots = main + owners * rem
    groups = PACK // rem if rem else 1
    levels = copies // 2
    rows = width // copies
    parts = PARTS
    others = owners - 1
    vmem = pl.BlockSpec(memory_space=pltpu.VMEM)
    hbm = pl.BlockSpec(memory_space=pl.ANY)
    dma = pltpu.SemaphoreType.DMA
    weight = pltpu.VMEM((width, ff), BF16)
    wide = pltpu.VMEM((slots, width), BF16)
    back = pltpu.VMEM((main, width), BF16)
    turned = pltpu.VMEM((width, slots), BF16)
    narrow = pltpu.VMEM((slots, ff), BF16)
    stack = pltpu.VMEM((3 * levels, rows, ff), BF16)
    packed = pltpu.VMEM((4, owners * PACK, width // groups), BF16)
    grad = jax.ShapeDtypeStruct((1, rows, ff), F32)
    results = pl.pallas_call(
        functools.partial(moe_kernel, owners, copies, base, rem, parts),
        out_shape=(
            jax.ShapeDtypeStruct((tok_count, width), BF16),
            jax.ShapeDtypeStruct((tok_count, width), BF16),
            jax.ShapeDtypeStruct(gate_probs.shape[::-1], F32),
            grad, grad, grad,
        ),
        in_specs=[vmem, vmem, vmem, vmem, hbm, hbm, hbm],
        out_specs=(vmem,) * 6,
        scratch_shapes=[
            weight, weight, weight,
            pltpu.VMEM((main, tok_count), BF16),
            pltpu.VMEM((groups, owners * PACK, tok_count), BF16),
            pltpu.VMEM((tok_count, main), BF16),
            pltpu.VMEM((groups, tok_count, owners * PACK), BF16),
            wide, wide, wide, wide, wide, back, back,
            packed, packed,
            turned, turned, turned,
            pltpu.VMEM((slots, ff), F32), pltpu.VMEM((slots, ff), F32),
            narrow, pltpu.VMEM((2, slots, ff), BF16), pltpu.VMEM((2, slots, ff), BF16),
            stack, stack, stack,
            pltpu.VMEM((3 * levels + 3, rows, ff), BF16),
            pltpu.VMEM((rows, ff // parts), F32),
            dma((3,)),
            *[dma((levels * others,))] * 8,
            dma((4 * others,)), dma((4 * others,)),
            dma((levels * owners + 1,)), dma((levels * owners + 1,)),
            dma((2 * parts,)), dma((2 * parts,)),
            *[dma((3 * levels * parts,))] * 3,
            dma(((3 * levels + 3) * parts,)),
        ],
        compiler_params=pltpu.CompilerParams(
            collective_id=0, has_side_effects=True, vmem_limit_bytes=62 * 2**20
        ),
    )(expert_ids.T, gate_probs.T, tokens, upstream, w_gate, w_up, w_down)
    layer_out, grad_tokens, grad_probs, grad_gate, grad_up, grad_down = pl.pallas_call(
        copy_kernel,
        out_shape=[jax.ShapeDtypeStruct(r.shape, r.dtype) for r in results],
        in_specs=[hbm] * 6,
        out_specs=[hbm] * 6,
        scratch_shapes=[pltpu.VMEM(r.shape, r.dtype) for r in results] + [dma((12,))],
    )(*results)
    return (layer_out, grad_tokens, grad_probs.T, grad_gate, grad_up, grad_down)


PACK = 16
PARTS = 3


def solution(mesh):
    rows = P(("dp", "expert"), None)
    experts = P("expert", None, None)
    grads = P("expert", "dp", None)
    return jax.shard_map(
        per_device,
        mesh=mesh,
        in_specs=(rows, rows, rows, rows, experts, experts, experts),
        out_specs=(rows, rows, rows, grads, grads, grads),
        check_vma=False,
    )
```
